128 devices in a mesh: gx: 8 (over z, y_lo), gy: 16 (over x, y_hi, core).
Axes of the slice: x: 4, y: 4 (y_hi: 2, y_lo: 2; y = y_hi * 2 + y_lo), z: 4, core: 2. Of those that a mesh axis runs over, the one named last changes fastest.
Arguments:
- positions: float32 [3, 327680], P(None, ('gx', 'gy')), may hold values from 0 to 1
- velocities: float32 [3, 327680], P(None, ('gx', 'gy')), may hold values from -6 to 6
- block_order: int32 [128, 20], P(('gx', 'gy')), may hold values from 0 to 19, each once within a row
- flags: int32 [128, 20], P(('gx', 'gy')), may hold values from 0 to 1, as said below
- offsets: int32 [3, 3], replicated, may hold values from -1 to 1
- pixels: int32 [3, 327680], P(None, ('gx', 'gy')), may hold values from 0 to 1048575, as said below
Outputs:
- new_positions: float32 [3, 327680], P(None, ('gx', 'gy'))
- new_velocities: float32 [3, 327680], P(None, ('gx', 'gy'))
- maps: float32 [8192, 384], P(('gx', 'gy'))
The draws below stay inside these ranges and needn't reach their ends.
Inputs may be any that keep to these rules, and one draw needn't show every extreme that they name: `flags`: each row holds 1 to 5 ones, and some row holds exactly 5. `block_order`: each row is a permutation. Among the 2560 columns of one slab cell and one replica, every strip of 8192 consecutive pixels is named exactly 2560 / 128 times.
All inputs are finite; a program needn't handle non-finite values.
Results may differ from the reference program's by a relative error of at most 0.0028.
Values may be sent and summed in bfloat16 or wider, within the bound.
A program may use at most 448 MiB of HBM per device.

```python
import jax
import jax.numpy as jnp
from jax import lax

BLOCKS_DEV = 20
BLOCK_LEN = 128
MOVERS = 2
CROSS_MAX = 5
REPLICAS = 3
STRIP_ROWS = 64
PARTS_DEV = 2560
PARTICLES = 327680
MAP_ROWS = 8192
PIXELS = 1048576
N_GX = 8
N_GY = 16
DEVICES = 128


def draw_flags(key, part):
    count_key = jax.random.fold_in(key, 101)
    busy_key = jax.random.fold_in(key, 202)
    shuffle_key = jax.random.fold_in(key, 303)
    counts = jax.random.randint(count_key, (DEVICES,), 1, CROSS_MAX + 1)
    busiest = jax.random.randint(busy_key, (), 0, DEVICES)
    counts = jnp.where(jnp.arange(DEVICES) == busiest, CROSS_MAX, counts)
    device_keys = jax.random.split(shuffle_key, DEVICES)

    def shuffle_one(k):
        return jax.random.permutation(k, BLOCKS_DEV)
    shuffled = jax.vmap(shuffle_one)(device_keys)
    return (shuffled < counts[:, None]).astype(jnp.int32)


def draw_pixels(key, part):
    owner_key = jax.random.fold_in(key, 404)
    lane_key = jax.random.fold_in(key, 505)
    group_keys = jax.random.split(owner_key, REPLICAS * DEVICES)

    def shuffle_one(k):
        return jax.random.permutation(k, PARTS_DEV)
    shuffled = jax.vmap(shuffle_one)(group_keys)
    owners = (shuffled % DEVICES).astype(jnp.int32)
    strip_size = STRIP_ROWS * 128
    inside = jax.random.randint(lane_key, (REPLICAS * DEVICES, PARTS_DEV), 0, strip_size)
    return (owners * strip_size + inside).reshape(REPLICAS, PARTICLES).astype(jnp.int32)


def plant(values, own_key, low, high):
    dims = values.shape
    index_at = [jax.random.randint(jax.random.fold_in(own_key, axis), (), 0, dims[axis]) for axis in range(len(dims))]
    values = values.at[tuple(index_at)].set(low)
    longest = dims.index(max(dims))
    index_at[longest] = (index_at[longest] + 1) % dims[longest]
    return values.at[tuple(index_at)].set(high)


def level_of(rng, extent, cuts, low, largest):
    gain = 1.0
    for dim, blocks in cuts:
        steps = jax.random.uniform(jax.random.fold_in(jax.random.fold_in(rng, 6), dim), (blocks,), jnp.float32, low / len(cuts), largest / len(cuts))
        gain = gain * jnp.repeat(jnp.exp(steps), extent[dim] // blocks).reshape((-1,) + (1,) * (len(extent) - 1 - dim))
    return gain


def centred(own_key, shape, scale, bound, cuts=(), kind=jnp.bfloat16):
    loudness = level_of(own_key, shape, cuts, -0.22, 0.18) if cuts else 1.0
    result = jax.random.normal(own_key, shape, jnp.float32) * scale * loudness
    return jnp.minimum(jnp.maximum(result, -bound), bound).astype(kind)


def setup_inputs(seed: int = 0) -> dict:
    keys = jax.random.split(jax.random.key(seed), 7)
    positions = jnp.clip(1.0 * jax.random.uniform(keys[0], (3, PARTICLES), jnp.float32) ** level_of(keys[0], (3, PARTICLES), ((1, 128),), -0.2, 0.2), 0.0, 1.0)
    velocities = centred(keys[1], (3, PARTICLES), 1.0, 6.0, ((1, 128),), jnp.float32)
    block_order = jax.vmap(lambda own: jax.random.permutation(own, BLOCKS_DEV))(jax.random.split(keys[2], DEVICES)).reshape((DEVICES, BLOCKS_DEV)).astype(jnp.int32)
    flags = draw_flags(jax.random.fold_in(keys[6], 71), 0)
    offsets = plant(jax.random.randint(keys[4], (REPLICAS, 3), -1, 2), jax.random.fold_in(keys[4], 1), -1, 1).astype(jnp.int32)
    pixels = draw_pixels(jax.random.fold_in(keys[6], 71), 0)
    return {"positions": positions, "velocities": velocities, "block_order": block_order, "flags": flags, "offsets": offsets, "pixels": pixels}


time_step = 0.05
lane_count = 128

def sky_terms(shifted, speeds, live_mask):
    radius = lax.optimization_barrier(jnp.sum(shifted * shifted, axis=1))
    weight = 1.0 / (1.0 + radius)
    radial = lax.optimization_barrier(jnp.sum(speeds[None] * shifted, axis=1)) / jnp.sqrt(1.0 + radius)
    energy = lax.optimization_barrier(jnp.sum(speeds * speeds, axis=0)) / 3.0
    return jnp.stack([weight * live_mask, weight * radial * live_mask, weight * energy[None] * live_mask], axis=0).astype(jnp.bfloat16)

def reference(positions, velocities, block_order, flags, offsets, pixels):
    full_shape = (3, N_GX, N_GY, BLOCKS_DEV, BLOCK_LEN)
    places = positions.reshape(full_shape)
    speeds = velocities.reshape(full_shape)
    places = places + time_step * speeds
    ordering = jnp.broadcast_to(block_order.reshape(1, N_GX, N_GY, BLOCKS_DEV, 1), full_shape)
    places = jnp.take_along_axis(places, ordering, axis=3)
    speeds = jnp.take_along_axis(speeds, ordering, axis=3)
    unit_vec = jnp.eye(3, dtype=jnp.float32).reshape(3, 3, 1, 1, 1, 1)
    pieces_pos = [places[:, :, :, 4 * MOVERS:]]
    pieces_vel = [speeds[:, :, :, 4 * MOVERS:]]
    migrations = ((0, 1, 1, -1.0), (1, 1, -1, 1.0), (2, 2, 1, -1.0), (3, 2, -1, 1.0))
    for which_set, mesh_dim, roll_by, sign_step in migrations:
        first_block = which_set * MOVERS
        moved_pos = places[:, :, :, first_block:first_block + MOVERS] + sign_step * unit_vec[mesh_dim - 1]
        pieces_pos.append(jnp.roll(moved_pos, roll_by, axis=mesh_dim))
        pieces_vel.append(jnp.roll(speeds[:, :, :, first_block:first_block + MOVERS], roll_by, axis=mesh_dim))
    places = jnp.concatenate(pieces_pos, axis=3)
    speeds = jnp.concatenate(pieces_vel, axis=3)
    cell_x = jnp.arange(N_GX, dtype=jnp.float32).reshape(1, N_GX, 1, 1, 1)
    cell_y = jnp.arange(N_GY, dtype=jnp.float32).reshape(1, 1, N_GY, 1, 1)
    global_pos = jnp.concatenate([(cell_x + places[0:1]) / N_GX, (cell_y + places[1:2]) / N_GY, places[2:3]], axis=0)
    global_flat = global_pos.reshape(3, PARTICLES)
    speed_flat = speeds.reshape(3, PARTICLES)
    live_mask = jnp.broadcast_to(flags.reshape(DEVICES, BLOCKS_DEV, 1), (DEVICES, BLOCKS_DEV, BLOCK_LEN)).reshape(PARTICLES).astype(jnp.float32)
    shifted = global_flat[None] + offsets.astype(jnp.float32)[:, :, None]
    values = sky_terms(shifted, speed_flat, live_mask)
    flat_values = values.reshape(3, REPLICAS * PARTICLES).T.astype(jnp.float32)
    summed = jax.ops.segment_sum(flat_values, pixels.reshape(REPLICAS * PARTICLES), num_segments=PIXELS)
    maps = jnp.transpose(summed.reshape(MAP_ROWS, lane_count, 3), (0, 2, 1)).reshape(MAP_ROWS, 3 * lane_count)
    return (places.reshape(3, PARTICLES), speeds.reshape(3, PARTICLES), maps)
```

```python
import jax
import jax.numpy as jnp
from jax import lax
from jax.sharding import PartitionSpec as P

MOVERS = 2
CROSS_MAX = 5
REPLICAS = 3
STRIP_ROWS = 64


time_step = 0.05
lane_count = 128


def passed_along(block, axis, distance):
    devices = range(lax.axis_size(axis))
    route = [((i - distance) % len(devices), i) for i in devices]
    return lax.ppermute(block, axis, route)


def sky_terms(shifted, speeds, live_mask):
    radius = jnp.sum(shifted * shifted, axis=1)
    weight = 1.0 / (1.0 + radius)
    radial = jnp.sum(speeds[None] * shifted, axis=1) / jnp.sqrt(1.0 + radius)
    energy = jnp.sum(speeds * speeds, axis=0) / 3.0
    return jnp.stack(
        [weight * live_mask, weight * radial * live_mask, weight * energy[None] * live_mask], axis=0
    ).astype(jnp.bfloat16)


def on_device(positions, velocities, block_order, flags, offsets, pixels):
    blocks = block_order.shape[1]
    width = positions.shape[1] // blocks
    places = positions.reshape(3, blocks, width)
    speeds = velocities.reshape(3, blocks, width)
    places = places + time_step * speeds
    ordering = block_order[0]
    places = jnp.take(places, ordering, axis=1)
    speeds = jnp.take(speeds, ordering, axis=1)

    def leaving(which_set, component, sign_step):
        first_block = which_set * MOVERS
        moved_pos = places[:, first_block : first_block + MOVERS].at[component].add(sign_step)
        return (moved_pos, speeds[:, first_block : first_block + MOVERS])

    east_pos, east_vel = leaving(0, 0, -1.0)
    from_west = passed_along((east_pos, east_vel), "gx", 1)
    west_pos, west_vel = leaving(1, 0, 1.0)
    from_east = passed_along((west_pos, west_vel), "gx", -1)
    north_pos, north_vel = leaving(2, 1, -1.0)
    from_south = passed_along((north_pos, north_vel), "gy", 1)
    south_pos, south_vel = leaving(3, 1, 1.0)
    from_north = passed_along((south_pos, south_vel), "gy", -1)
    arrived = (from_west, from_east, from_south, from_north)
    new_places = jnp.concatenate(
        [places[:, 4 * MOVERS :]] + [received[0] for received in arrived], axis=1
    )
    new_speeds = jnp.concatenate(
        [speeds[:, 4 * MOVERS :]] + [received[1] for received in arrived], axis=1
    )
    count_x = lax.axis_size("gx")
    count_y = lax.axis_size("gy")
    devices = count_x * count_y
    cell_x = lax.axis_index("gx")
    cell_y = lax.axis_index("gy")
    flag_row = flags[0]
    ranking = (1 - flag_row) * blocks + jnp.arange(blocks, dtype=jnp.int32)
    chosen = jnp.argsort(ranking)[:CROSS_MAX]
    live_mask = jnp.take(flag_row, chosen).astype(jnp.float32).reshape(1, CROSS_MAX, 1)
    picked_pos = jnp.take(new_places, chosen, axis=1)
    picked_vel = jnp.take(new_speeds, chosen, axis=1)
    picked_ids = jnp.take(pixels.reshape(REPLICAS, blocks, width), chosen, axis=1)
    global_pos = jnp.stack(
        [
            (cell_x.astype(jnp.float32) + picked_pos[0]) / count_x,
            (cell_y.astype(jnp.float32) + picked_pos[1]) / count_y,
            picked_pos[2],
        ],
        axis=0,
    )
    shifted = global_pos[None] + offsets.astype(jnp.float32)[:, :, None, None]
    values = sky_terms(shifted, picked_vel, live_mask)

    strip_size = STRIP_ROWS * lane_count
    per_replica = CROSS_MAX * width
    ids = picked_ids.reshape(REPLICAS, per_replica)
    dest = ids // strip_size
    inside = ids % strip_size
    order = jnp.arange(per_replica, dtype=jnp.int32)
    same = (dest[:, :, None] == dest[:, None, :]) & (order[None, None, :] < order[None, :, None])
    rank = jnp.sum(same.astype(jnp.int32), axis=2)
    slots = REPLICAS * blocks
    slot = dest * slots + jnp.arange(REPLICAS, dtype=jnp.int32)[:, None] * blocks + rank
    fields = jnp.concatenate(
        [
            jnp.transpose(values.reshape(3, REPLICAS, per_replica), (1, 2, 0)),
            (inside // lane_count).astype(jnp.bfloat16)[:, :, None],
            (inside % lane_count).astype(jnp.bfloat16)[:, :, None],
        ],
        axis=2,
    ).reshape(REPLICAS * per_replica, 5)
    send = jnp.zeros((devices * slots, 5), jnp.bfloat16)
    send = send.at[slot.reshape(-1)].set(fields, unique_indices=True, mode="promise_in_bounds")
    send = send.reshape(devices, slots, 5)
    got = lax.all_to_all(send, ("gx", "gy"), 0, 0, tiled=True).reshape(devices * slots, 5)

    rows = got[:, 3].astype(jnp.int32)
    lanes = got[:, 4].astype(jnp.int32)
    row_hits = (rows[None, :] == jnp.arange(STRIP_ROWS, dtype=jnp.int32)[:, None]).astype(jnp.bfloat16)
    lane_hits = (lanes[:, None] == jnp.arange(lane_count, dtype=jnp.int32)[None, :]).astype(jnp.bfloat16)
    spread = (got[:, :3, None] * lane_hits[:, None, :]).reshape(devices * slots, 3 * lane_count)
    maps = jnp.dot(row_hits, spread, preferred_element_type=jnp.float32)
    return (new_places.reshape(3, blocks * width), new_speeds.reshape(3, blocks * width), maps)


def solution(mesh):
    in_specs = (
        P(None, ("gx", "gy")),
        P(None, ("gx", "gy")),
        P(("gx", "gy"), None),
        P(("gx", "gy"), None),
        P(),
        P(None, ("gx", "gy")),
    )
    out_specs = (P(None, ("gx", "gy")), P(None, ("gx", "gy")), P(("gx", "gy"), None))
    return jax.shard_map(
        on_device, mesh=mesh, in_specs=in_specs, out_specs=out_specs, check_vma=False
    )
```

```python
import jax
import jax.numpy as jnp
from jax import lax
from jax.sharding import PartitionSpec as P

MOVERS = 2
CROSS_MAX = 5
REPLICAS = 3
STRIP_ROWS = 64


time_step = 0.05
lane_count = 128


def passed_along(block, axis, distance):
    devices = range(lax.axis_size(axis))
    route = [((i - distance) % len(devices), i) for i in devices]
    return lax.ppermute(block, axis, route)


def sky_terms(shifted, speeds, live_mask):
    radius = jnp.sum(shifted * shifted, axis=1)
    weight = 1.0 / (1.0 + radius)
    radial = jnp.sum(speeds[None] * shifted, axis=1) / jnp.sqrt(1.0 + radius)
    energy = jnp.sum(speeds * speeds, axis=0) / 3.0
    return jnp.stack(
        [weight * live_mask, weight * radial * live_mask, weight * energy[None] * live_mask], axis=0
    ).astype(jnp.bfloat16)


def on_device(positions, velocities, block_order, flags, offsets, pixels):
    blocks = block_order.shape[1]
    width = positions.shape[1] // blocks
    places = positions.reshape(3, blocks, width)
    speeds = velocities.reshape(3, blocks, width)
    places = places + time_step * speeds
    ordering = block_order[0]
    places = jnp.take(places, ordering, axis=1)
    speeds = jnp.take(speeds, ordering, axis=1)

    def leaving(which_set, component, sign_step):
        first_block = which_set * MOVERS
        moved_pos = places[:, first_block : first_block + MOVERS].at[component].add(sign_step)
        return (moved_pos, speeds[:, first_block : first_block + MOVERS])

    def moved(which_set, component, sign_step, axis, distance):
        pos, vel = leaving(which_set, component, sign_step)
        got = passed_along(jnp.concatenate([pos, vel], axis=0), axis, distance)
        return got[:3], got[3:]

    arrived = (
        moved(0, 0, -1.0, "gx", 1),
        moved(1, 0, 1.0, "gx", -1),
        moved(2, 1, -1.0, "gy", 1),
        moved(3, 1, 1.0, "gy", -1),
    )
    new_places = jnp.concatenate(
        [places[:, 4 * MOVERS :]] + [received[0] for received in arrived], axis=1
    )
    new_speeds = jnp.concatenate(
        [speeds[:, 4 * MOVERS :]] + [received[1] for received in arrived], axis=1
    )
    count_x = lax.axis_size("gx")
    count_y = lax.axis_size("gy")
    devices = count_x * count_y
    cell_x = lax.axis_index("gx")
    cell_y = lax.axis_index("gy")
    flag_row = flags[0]
    ranking = (1 - flag_row) * blocks + jnp.arange(blocks, dtype=jnp.int32)
    chosen = jnp.argsort(ranking)[:CROSS_MAX]
    live_mask = jnp.take(flag_row, chosen).astype(jnp.float32).reshape(1, CROSS_MAX, 1)
    picked_pos = jnp.take(new_places, chosen, axis=1)
    picked_vel = jnp.take(new_speeds, chosen, axis=1)
    picked_ids = jnp.take(pixels.reshape(REPLICAS, blocks, width), chosen, axis=1)
    global_pos = jnp.stack(
        [
            (cell_x.astype(jnp.float32) + picked_pos[0]) / count_x,
            (cell_y.astype(jnp.float32) + picked_pos[1]) / count_y,
            picked_pos[2],
        ],
        axis=0,
    )
    shifted = global_pos[None] + offsets.astype(jnp.float32)[:, :, None, None]
    values = sky_terms(shifted, picked_vel, live_mask)

    strip_size = STRIP_ROWS * lane_count
    per_replica = CROSS_MAX * width
    ids = picked_ids.reshape(REPLICAS, per_replica)
    dest = ids // strip_size
    inside = ids % strip_size
    order = jnp.arange(per_replica, dtype=jnp.int32)
    same = (dest[:, :, None] == dest[:, None, :]) & (order[None, None, :] < order[None, :, None])
    rank = jnp.sum(same.astype(jnp.int32), axis=2)
    slots = REPLICAS * blocks
    fields = jnp.concatenate(
        [
            jnp.transpose(values.reshape(3, REPLICAS, per_replica), (1, 2, 0)),
            (inside // lane_count).astype(jnp.bfloat16)[:, :, None],
            (inside % lane_count).astype(jnp.bfloat16)[:, :, None],
        ],
        axis=2,
    )
    dest_hits = (dest[:, :, None] == jnp.arange(devices, dtype=jnp.int32)).astype(jnp.bfloat16)
    rank_hits = (rank[:, :, None] == jnp.arange(blocks, dtype=jnp.int32)).astype(jnp.bfloat16)
    placed = (rank_hits[:, :, :, None] * fields[:, :, None, :]).reshape(REPLICAS, per_replica, blocks * 5)
    send = lax.dot_general(
        dest_hits, placed, (((1,), (1,)), ((0,), (0,))), preferred_element_type=jnp.float32
    ).astype(jnp.bfloat16)
    send = jnp.transpose(send, (1, 0, 2)).reshape(devices, slots, 5)
    got = lax.all_to_all(send, ("gx", "gy"), 0, 0, tiled=True).reshape(devices * slots, 5)

    rows = got[:, 3].astype(jnp.int32)
    lanes = got[:, 4].astype(jnp.int32)
    row_hits = (rows[None, :] == jnp.arange(STRIP_ROWS, dtype=jnp.int32)[:, None]).astype(jnp.bfloat16)
    lane_hits = (lanes[:, None] == jnp.arange(lane_count, dtype=jnp.int32)[None, :]).astype(jnp.bfloat16)
    spread = (got[:, :3, None] * lane_hits[:, None, :]).reshape(devices * slots, 3 * lane_count)
    maps = jnp.dot(row_hits, spread, preferred_element_type=jnp.float32)
    return (new_places.reshape(3, blocks * width), new_speeds.reshape(3, blocks * width), maps)


def solution(mesh):
    in_specs = (
        P(None, ("gx", "gy")),
        P(None, ("gx", "gy")),
        P(("gx", "gy"), None),
        P(("gx", "gy"), None),
        P(),
        P(None, ("gx", "gy")),
    )
    out_specs = (P(None, ("gx", "gy")), P(None, ("gx", "gy")), P(("gx", "gy"), None))
    return jax.shard_map(
        on_device, mesh=mesh, in_specs=in_specs, out_specs=out_specs, check_vma=False
    )
```

```python
import functools

import jax
import jax.numpy as jnp
from jax import lax
from jax.experimental import pallas as pl
from jax.experimental.pallas import tpu as pltpu
from jax.sharding import PartitionSpec as P

MOVERS = 2
CROSS_MAX = 5
REPLICAS = 3
STRIP_ROWS = 64


time_step = 0.05
lane_count = 128
FIELDS = 8
MESH = pl.DeviceIdType.MESH


def exchange_kernel(count_y, send_ref, maps_ref, recv, send_sem, recv_sem):
    devices = send_ref.shape[0]
    rows = maps_ref.shape[0]
    me = lax.axis_index("gx") * count_y + lax.axis_index("gy")

    def peer(offset):
        other = lax.rem(me + offset, devices)
        return other, (other // count_y, other % count_y)

    barrier = pltpu.get_barrier_semaphore()

    def greet(offset, carry):
        pl.semaphore_signal(barrier, 1, device_id=peer(offset)[1], device_id_type=MESH)
        return carry

    lax.fori_loop(1, devices, greet, 0)
    pl.semaphore_wait(barrier, devices - 1)
    pltpu.make_async_copy(send_ref.at[me], recv.at[me], recv_sem).start()

    def post(offset, carry):
        other, where = peer(offset)
        pltpu.make_async_remote_copy(
            src_ref=send_ref.at[other],
            dst_ref=recv.at[me],
            send_sem=send_sem,
            recv_sem=recv_sem,
            device_id=where,
            device_id_type=MESH,
        ).start()
        return carry

    lax.fori_loop(1, devices, post, 0)
    pltpu.make_async_copy(
        send_ref.at[pl.ds(0, devices - 1)], recv.at[pl.ds(0, devices - 1)], send_sem
    ).wait()
    pltpu.make_async_copy(send_ref, recv, recv_sem).wait()

    row_iota = lax.broadcasted_iota(jnp.int32, (rows, lane_count), 0)
    lane_iota = lax.broadcasted_iota(jnp.int32, (lane_count, lane_count), 0)

    def deposit(source, total):
        chunk = recv[source]
        row_hits = (chunk[3:4, :].astype(jnp.int32) == row_iota).astype(jnp.bfloat16)
        lane_hits = chunk[4:5, :].astype(jnp.int32) == lane_iota
        spread = jnp.concatenate(
            [jnp.where(lane_hits, chunk[c : c + 1, :], 0.0) for c in range(3)], axis=0
        ).astype(jnp.bfloat16)
        return total + lax.dot_general(
            row_hits, spread, (((1,), (1,)), ((), ())), preferred_element_type=jnp.float32
        )

    maps_ref[...] = lax.fori_loop(
        0, devices, deposit, jnp.zeros(maps_ref.shape, jnp.float32)
    )


def exchange(send, count_y):
    devices = send.shape[0]
    return pl.pallas_call(
        functools.partial(exchange_kernel, count_y),
        out_shape=jax.ShapeDtypeStruct((STRIP_ROWS, 3 * lane_count), jnp.float32),
        in_specs=[pl.BlockSpec(memory_space=pltpu.VMEM)],
        out_specs=pl.BlockSpec(memory_space=pltpu.VMEM),
        scratch_shapes=[
            pltpu.VMEM(send.shape, jnp.float32),
            pltpu.SemaphoreType.DMA(()),
            pltpu.SemaphoreType.DMA(()),
        ],
        compiler_params=pltpu.CompilerParams(collective_id=0, has_side_effects=True),
    )(send)


def passed_along(block, axis, distance):
    devices = range(lax.axis_size(axis))
    route = [((i - distance) % len(devices), i) for i in devices]
    return lax.ppermute(block, axis, route)


def sky_terms(shifted, speeds, live_mask):
    radius = jnp.sum(shifted * shifted, axis=1)
    weight = 1.0 / (1.0 + radius)
    radial = jnp.sum(speeds[None] * shifted, axis=1) / jnp.sqrt(1.0 + radius)
    energy = jnp.sum(speeds * speeds, axis=0) / 3.0
    return jnp.stack(
        [weight * live_mask, weight * radial * live_mask, weight * energy[None] * live_mask], axis=0
    ).astype(jnp.bfloat16)


def on_device(positions, velocities, block_order, flags, offsets, pixels):
    blocks = block_order.shape[1]
    width = positions.shape[1] // blocks
    places = positions.reshape(3, blocks, width)
    speeds = velocities.reshape(3, blocks, width)
    places = places + time_step * speeds
    ordering = block_order[0]
    places = jnp.take(places, ordering, axis=1)
    speeds = jnp.take(speeds, ordering, axis=1)

    def leaving(which_set, component, sign_step):
        first_block = which_set * MOVERS
        moved_pos = places[:, first_block : first_block + MOVERS].at[component].add(sign_step)
        return (moved_pos, speeds[:, first_block : first_block + MOVERS])

    def moved(which_set, component, sign_step, axis, distance):
        pos, vel = leaving(which_set, component, sign_step)
        got = passed_along(jnp.concatenate([pos, vel], axis=0), axis, distance)
        return got[:3], got[3:]

    arrived = (
        moved(0, 0, -1.0, "gx", 1),
        moved(1, 0, 1.0, "gx", -1),
        moved(2, 1, -1.0, "gy", 1),
        moved(3, 1, 1.0, "gy", -1),
    )
    new_places = jnp.concatenate(
        [places[:, 4 * MOVERS :]] + [received[0] for received in arrived], axis=1
    )
    new_speeds = jnp.concatenate(
        [speeds[:, 4 * MOVERS :]] + [received[1] for received in arrived], axis=1
    )
    count_x = lax.axis_size("gx")
    count_y = lax.axis_size("gy")
    devices = count_x * count_y
    cell_x = lax.axis_index("gx")
    cell_y = lax.axis_index("gy")
    flag_row = flags[0]
    ranking = (1 - flag_row) * blocks + jnp.arange(blocks, dtype=jnp.int32)
    chosen = jnp.argsort(ranking)[:CROSS_MAX]
    live_mask = jnp.take(flag_row, chosen).astype(jnp.float32).reshape(1, CROSS_MAX, 1)
    picked_pos = jnp.take(new_places, chosen, axis=1)
    picked_vel = jnp.take(new_speeds, chosen, axis=1)
    picked_ids = jnp.take(pixels.reshape(REPLICAS, blocks, width), chosen, axis=1)
    global_pos = jnp.stack(
        [
            (cell_x.astype(jnp.float32) + picked_pos[0]) / count_x,
            (cell_y.astype(jnp.float32) + picked_pos[1]) / count_y,
            picked_pos[2],
        ],
        axis=0,
    )
    shifted = global_pos[None] + offsets.astype(jnp.float32)[:, :, None, None]
    values = sky_terms(shifted, picked_vel, live_mask)

    strip_size = STRIP_ROWS * lane_count
    per_replica = CROSS_MAX * width
    ids = picked_ids.reshape(REPLICAS, per_replica)
    dest = ids // strip_size
    inside = ids % strip_size
    order = jnp.arange(per_replica, dtype=jnp.int32)
    same = (dest[:, :, None] == dest[:, None, :]) & (order[None, None, :] < order[None, :, None])
    rank = jnp.sum(same.astype(jnp.int32), axis=2)
    slots = REPLICAS * blocks
    fields = jnp.concatenate(
        [
            jnp.transpose(values.reshape(3, REPLICAS, per_replica), (1, 2, 0)),
            (inside // lane_count).astype(jnp.bfloat16)[:, :, None],
            (inside % lane_count).astype(jnp.bfloat16)[:, :, None],
        ],
        axis=2,
    )
    dest_hits = (dest[:, :, None] == jnp.arange(devices, dtype=jnp.int32)).astype(jnp.bfloat16)
    rank_hits = (rank[:, :, None] == jnp.arange(blocks, dtype=jnp.int32)).astype(jnp.bfloat16)
    placed = (fields[:, :, :, None] * rank_hits[:, :, None, :]).reshape(REPLICAS, per_replica, 5 * blocks)
    send = lax.dot_general(
        dest_hits, placed, (((1,), (1,)), ((0,), (0,))), preferred_element_type=jnp.float32
    )
    send = jnp.transpose(send.reshape(REPLICAS, devices, 5, blocks), (1, 2, 0, 3))
    send = send.reshape(devices, 5, slots)
    send = jnp.pad(send, ((0, 0), (0, FIELDS - 5), (0, lane_count - slots)))
    maps = exchange(send, count_y)
    return (new_places.reshape(3, blocks * width), new_speeds.reshape(3, blocks * width), maps)


def solution(mesh):
    in_specs = (
        P(None, ("gx", "gy")),
        P(None, ("gx", "gy")),
        P(("gx", "gy"), None),
        P(("gx", "gy"), None),
        P(),
        P(None, ("gx", "gy")),
    )
    out_specs = (P(None, ("gx", "gy")), P(None, ("gx", "gy")), P(("gx", "gy"), None))
    return jax.shard_map(
        on_device, mesh=mesh, in_specs=in_specs, out_specs=out_specs, check_vma=False
    )
```

```python
import functools

import jax
import jax.numpy as jnp
from jax import lax
from jax.experimental import pallas as pl
from jax.experimental.pallas import tpu as pltpu
from jax.sharding import PartitionSpec as P

MOVERS = 2
CROSS_MAX = 5
REPLICAS = 3
STRIP_ROWS = 64


time_step = 0.05
lane_count = 128
MESH = pl.DeviceIdType.MESH


def exchange_kernel(count_y, send_ref, out_ref, recv, send_sem, recv_sem):
    devices = send_ref.shape[0]
    me = lax.axis_index("gx") * count_y + lax.axis_index("gy")

    def peer(offset):
        other = lax.rem(me + offset, devices)
        return other, (other // count_y, other % count_y)

    barrier = pltpu.get_barrier_semaphore()

    def greet(offset, carry):
        pl.semaphore_signal(barrier, 1, device_id=peer(offset)[1], device_id_type=MESH)
        return carry

    lax.fori_loop(1, devices, greet, 0)
    pl.semaphore_wait(barrier, devices - 1)
    pltpu.make_async_copy(send_ref.at[me], recv.at[me], recv_sem).start()

    def post(offset, carry):
        other, where = peer(offset)
        pltpu.make_async_remote_copy(
            src_ref=send_ref.at[other],
            dst_ref=recv.at[me],
            send_sem=send_sem,
            recv_sem=recv_sem,
            device_id=where,
            device_id_type=MESH,
        ).start()
        return carry

    lax.fori_loop(1, devices, post, 0)
    pltpu.make_async_copy(
        send_ref.at[pl.ds(0, devices - 1)], recv.at[pl.ds(0, devices - 1)], send_sem
    ).wait()
    pltpu.make_async_copy(send_ref, recv, recv_sem).wait()

    out_ref[...] = recv[...]


def exchange(send, count_y):
    devices = send.shape[0]
    return pl.pallas_call(
        functools.partial(exchange_kernel, count_y),
        out_shape=jax.ShapeDtypeStruct(send.shape, jnp.float32),
        in_specs=[pl.BlockSpec(memory_space=pltpu.VMEM)],
        out_specs=pl.BlockSpec(memory_space=pltpu.VMEM),
        scratch_shapes=[
            pltpu.VMEM(send.shape, jnp.float32),
            pltpu.SemaphoreType.DMA(()),
            pltpu.SemaphoreType.DMA(()),
        ],
        compiler_params=pltpu.CompilerParams(collective_id=0, has_side_effects=True),
    )(send)


def passed_along(block, axis, distance):
    devices = range(lax.axis_size(axis))
    route = [((i - distance) % len(devices), i) for i in devices]
    return lax.ppermute(block, axis, route)


def sky_terms(shifted, speeds, live_mask):
    radius = jnp.sum(shifted * shifted, axis=1)
    weight = 1.0 / (1.0 + radius)
    radial = jnp.sum(speeds[None] * shifted, axis=1) / jnp.sqrt(1.0 + radius)
    energy = jnp.sum(speeds * speeds, axis=0) / 3.0
    return jnp.stack(
        [weight * live_mask, weight * radial * live_mask, weight * energy[None] * live_mask], axis=0
    ).astype(jnp.bfloat16)


def on_device(positions, velocities, block_order, flags, offsets, pixels):
    blocks = block_order.shape[1]
    width = positions.shape[1] // blocks
    places = positions.reshape(3, blocks, width)
    speeds = velocities.reshape(3, blocks, width)
    places = places + time_step * speeds
    ordering = block_order[0]
    places = jnp.take(places, ordering, axis=1)
    speeds = jnp.take(speeds, ordering, axis=1)

    def leaving(which_set, component, sign_step):
        first_block = which_set * MOVERS
        moved_pos = places[:, first_block : first_block + MOVERS].at[component].add(sign_step)
        return (moved_pos, speeds[:, first_block : first_block + MOVERS])

    def moved(which_set, component, sign_step, axis, distance):
        pos, vel = leaving(which_set, component, sign_step)
        got = passed_along(jnp.concatenate([pos, vel], axis=0), axis, distance)
        return got[:3], got[3:]

    arrived = (
        moved(0, 0, -1.0, "gx", 1),
        moved(1, 0, 1.0, "gx", -1),
        moved(2, 1, -1.0, "gy", 1),
        moved(3, 1, 1.0, "gy", -1),
    )
    new_places = jnp.concatenate(
        [places[:, 4 * MOVERS :]] + [received[0] for received in arrived], axis=1
    )
    new_speeds = jnp.concatenate(
        [speeds[:, 4 * MOVERS :]] + [received[1] for received in arrived], axis=1
    )
    count_x = lax.axis_size("gx")
    count_y = lax.axis_size("gy")
    devices = count_x * count_y
    cell_x = lax.axis_index("gx")
    cell_y = lax.axis_index("gy")
    flag_row = flags[0]
    ranking = (1 - flag_row) * blocks + jnp.arange(blocks, dtype=jnp.int32)
    chosen = jnp.argsort(ranking)[:CROSS_MAX]
    live_mask = jnp.take(flag_row, chosen).astype(jnp.float32).reshape(1, CROSS_MAX, 1)
    picked_pos = jnp.take(new_places, chosen, axis=1)
    picked_vel = jnp.take(new_speeds, chosen, axis=1)
    picked_ids = jnp.take(pixels.reshape(REPLICAS, blocks, width), chosen, axis=1)
    global_pos = jnp.stack(
        [
            (cell_x.astype(jnp.float32) + picked_pos[0]) / count_x,
            (cell_y.astype(jnp.float32) + picked_pos[1]) / count_y,
            picked_pos[2],
        ],
        axis=0,
    )
    shifted = global_pos[None] + offsets.astype(jnp.float32)[:, :, None, None]
    values = sky_terms(shifted, picked_vel, live_mask)

    strip_size = STRIP_ROWS * lane_count
    per_replica = CROSS_MAX * width
    ids = picked_ids.reshape(REPLICAS, per_replica)
    dest = ids // strip_size
    inside = ids % strip_size
    order = jnp.arange(per_replica, dtype=jnp.int32)
    same = (dest[:, :, None] == dest[:, None, :]) & (order[None, None, :] < order[None, :, None])
    rank = jnp.sum(same.astype(jnp.int32), axis=2)
    slots = REPLICAS * blocks
    fields = jnp.concatenate(
        [
            jnp.transpose(values.reshape(3, REPLICAS, per_replica), (1, 2, 0)),
            (inside // lane_count).astype(jnp.bfloat16)[:, :, None],
            (inside % lane_count).astype(jnp.bfloat16)[:, :, None],
        ],
        axis=2,
    )
    dest_hits = (dest[:, :, None] == jnp.arange(devices, dtype=jnp.int32)).astype(jnp.bfloat16)
    rank_hits = (rank[:, :, None] == jnp.arange(blocks, dtype=jnp.int32)).astype(jnp.bfloat16)
    placed = (fields[:, :, :, None] * rank_hits[:, :, None, :]).reshape(REPLICAS, per_replica, 5 * blocks)
    send = lax.dot_general(
        dest_hits, placed, (((1,), (1,)), ((0,), (0,))), preferred_element_type=jnp.float32
    )
    send = jnp.transpose(send.reshape(REPLICAS, devices, 5, blocks), (1, 2, 0, 3))
    send = send.reshape(devices, 5, slots)
    pixel = send[:, 3] * lane_count + send[:, 4]
    half = lane_count // 2
    pad = ((0, 0), (0, half - slots))
    send = jnp.stack(
        [
            jnp.concatenate([jnp.pad(send[:, 0], pad), jnp.pad(send[:, 1], pad)], axis=1),
            jnp.concatenate([jnp.pad(send[:, 2], pad), jnp.pad(pixel, pad)], axis=1),
        ],
        axis=1,
    )
    got = exchange(send, count_y)
    got_values = jnp.stack([got[:, 0, :half], got[:, 0, half:], got[:, 1, :half]], axis=1)
    got_values = got_values.reshape(devices, 3, half).transpose(0, 2, 1).reshape(devices * half, 3)
    got_pixel = got[:, 1, half:].reshape(devices * half).astype(jnp.int32)
    rows = got_pixel // lane_count
    lanes = got_pixel % lane_count
    row_hits = (rows[None, :] == jnp.arange(STRIP_ROWS, dtype=jnp.int32)[:, None]).astype(jnp.bfloat16)
    lane_hits = (lanes[:, None] == jnp.arange(lane_count, dtype=jnp.int32)[None, :]).astype(jnp.bfloat16)
    spread = (got_values.astype(jnp.bfloat16)[:, :, None] * lane_hits[:, None, :]).reshape(
        devices * half, 3 * lane_count
    )
    maps = jnp.dot(row_hits, spread, preferred_element_type=jnp.float32)
    return (new_places.reshape(3, blocks * width), new_speeds.reshape(3, blocks * width), maps)


def solution(mesh):
    in_specs = (
        P(None, ("gx", "gy")),
        P(None, ("gx", "gy")),
        P(("gx", "gy"), None),
        P(("gx", "gy"), None),
        P(),
        P(None, ("gx", "gy")),
    )
    out_specs = (P(None, ("gx", "gy")), P(None, ("gx", "gy")), P(("gx", "gy"), None))
    return jax.shard_map(
        on_device, mesh=mesh, in_specs=in_specs, out_specs=out_specs, check_vma=False
    )
```

```python
import functools

import jax
import jax.numpy as jnp
from jax import lax
from jax.experimental import pallas as pl
from jax.experimental.pallas import tpu as pltpu
from jax.sharding import PartitionSpec as P

MOVERS = 2
CROSS_MAX = 5
REPLICAS = 3
STRIP_ROWS = 64


time_step = 0.05
lane_count = 128
MESH = pl.DeviceIdType.MESH


def exchange_kernel(count_y, send_ref, out_ref, recv, send_sem, recv_sem):
    devices = send_ref.shape[0]
    me = lax.axis_index("gx") * count_y + lax.axis_index("gy")

    def peer(offset):
        other = lax.rem(me + offset, devices)
        return other, (other // count_y, other % count_y)

    barrier = pltpu.get_barrier_semaphore()

    def greet(offset, carry):
        pl.semaphore_signal(barrier, 1, device_id=peer(offset)[1], device_id_type=MESH)
        return carry

    lax.fori_loop(1, devices, greet, 0)
    pl.semaphore_wait(barrier, devices - 1)
    pltpu.make_async_copy(send_ref.at[me], recv.at[me], recv_sem).start()

    def post(offset, carry):
        other, where = peer(offset)
        pltpu.make_async_remote_copy(
            src_ref=send_ref.at[other],
            dst_ref=recv.at[me],
            send_sem=send_sem,
            recv_sem=recv_sem,
            device_id=where,
            device_id_type=MESH,
        ).start()
        return carry

    lax.fori_loop(1, devices, post, 0)
    pltpu.make_async_copy(
        send_ref.at[pl.ds(0, devices - 1)], recv.at[pl.ds(0, devices - 1)], send_sem
    ).wait()
    pltpu.make_async_copy(send_ref, recv, recv_sem).wait()

    out_ref[...] = recv[...]


def migrate_kernel(send_ref, out_ref, recv, send_sem, recv_sem):
    count_x = lax.axis_size("gx")
    count_y = lax.axis_size("gy")
    x = lax.axis_index("gx")
    y = lax.axis_index("gy")
    faces = (
        (lax.rem(x + 1, count_x), y),
        (lax.rem(x + count_x - 1, count_x), y),
        (x, lax.rem(y + 1, count_y)),
        (x, lax.rem(y + count_y - 1, count_y)),
    )
    barrier = pltpu.get_barrier_semaphore()
    for where in faces:
        pl.semaphore_signal(barrier, 1, device_id=where, device_id_type=MESH)
    pl.semaphore_wait(barrier, len(faces))
    copies = []
    for face, where in enumerate(faces):
        copy = pltpu.make_async_remote_copy(
            src_ref=send_ref.at[face],
            dst_ref=recv.at[face],
            send_sem=send_sem.at[face],
            recv_sem=recv_sem.at[face],
            device_id=where,
            device_id_type=MESH,
        )
        copy.start()
        copies.append(copy)
    for copy in copies:
        copy.wait()
    out_ref[...] = recv[...]


def migrate(leaving):
    faces = leaving.shape[0]
    return pl.pallas_call(
        migrate_kernel,
        out_shape=jax.ShapeDtypeStruct(leaving.shape, jnp.float32),
        in_specs=[pl.BlockSpec(memory_space=pltpu.VMEM)],
        out_specs=pl.BlockSpec(memory_space=pltpu.VMEM),
        scratch_shapes=[
            pltpu.VMEM(leaving.shape, jnp.float32),
            pltpu.SemaphoreType.DMA((faces,)),
            pltpu.SemaphoreType.DMA((faces,)),
        ],
        compiler_params=pltpu.CompilerParams(collective_id=1, has_side_effects=True),
    )(leaving)


def exchange(send, count_y):
    devices = send.shape[0]
    return pl.pallas_call(
        functools.partial(exchange_kernel, count_y),
        out_shape=jax.ShapeDtypeStruct(send.shape, jnp.float32),
        in_specs=[pl.BlockSpec(memory_space=pltpu.VMEM)],
        out_specs=pl.BlockSpec(memory_space=pltpu.VMEM),
        scratch_shapes=[
            pltpu.VMEM(send.shape, jnp.float32),
            pltpu.SemaphoreType.DMA(()),
            pltpu.SemaphoreType.DMA(()),
        ],
        compiler_params=pltpu.CompilerParams(collective_id=0, has_side_effects=True),
    )(send)


def sky_terms(shifted, speeds, live_mask):
    radius = jnp.sum(shifted * shifted, axis=1)
    weight = 1.0 / (1.0 + radius)
    radial = jnp.sum(speeds[None] * shifted, axis=1) / jnp.sqrt(1.0 + radius)
    energy = jnp.sum(speeds * speeds, axis=0) / 3.0
    return jnp.stack(
        [weight * live_mask, weight * radial * live_mask, weight * energy[None] * live_mask], axis=0
    ).astype(jnp.bfloat16)


def on_device(positions, velocities, block_order, flags, offsets, pixels):
    blocks = block_order.shape[1]
    width = positions.shape[1] // blocks
    places = positions.reshape(3, blocks, width)
    speeds = velocities.reshape(3, blocks, width)
    places = places + time_step * speeds
    ordering = block_order[0]
    places = jnp.take(places, ordering, axis=1)
    speeds = jnp.take(speeds, ordering, axis=1)

    def leaving(which_set, component, sign_step):
        first_block = which_set * MOVERS
        moved_pos = places[:, first_block : first_block + MOVERS].at[component].add(sign_step)
        return (moved_pos, speeds[:, first_block : first_block + MOVERS])

    leaving_sets = ((0, 0, -1.0), (1, 0, 1.0), (2, 1, -1.0), (3, 1, 1.0))
    leaving_blocks = jnp.stack(
        [jnp.concatenate(leaving(*face), axis=0) for face in leaving_sets], axis=0
    ).reshape(4, 6, MOVERS * width)
    got_faces = migrate(leaving_blocks).reshape(4, 6, MOVERS, width)
    arrived = [(got_faces[face, :3], got_faces[face, 3:]) for face in range(4)]
    new_places = jnp.concatenate(
        [places[:, 4 * MOVERS :]] + [received[0] for received in arrived], axis=1
    )
    new_speeds = jnp.concatenate(
        [speeds[:, 4 * MOVERS :]] + [received[1] for received in arrived], axis=1
    )
    count_x = lax.axis_size("gx")
    count_y = lax.axis_size("gy")
    devices = count_x * count_y
    cell_x = lax.axis_index("gx")
    cell_y = lax.axis_index("gy")
    flag_row = flags[0]
    ranking = (1 - flag_row) * blocks + jnp.arange(blocks, dtype=jnp.int32)
    chosen = jnp.argsort(ranking)[:CROSS_MAX]
    live_mask = jnp.take(flag_row, chosen).astype(jnp.float32).reshape(1, CROSS_MAX, 1)
    picked_pos = jnp.take(new_places, chosen, axis=1)
    picked_vel = jnp.take(new_speeds, chosen, axis=1)
    picked_ids = jnp.take(pixels.reshape(REPLICAS, blocks, width), chosen, axis=1)
    global_pos = jnp.stack(
        [
            (cell_x.astype(jnp.float32) + picked_pos[0]) / count_x,
            (cell_y.astype(jnp.float32) + picked_pos[1]) / count_y,
            picked_pos[2],
        ],
        axis=0,
    )
    shifted = global_pos[None] + offsets.astype(jnp.float32)[:, :, None, None]
    values = sky_terms(shifted, picked_vel, live_mask)

    strip_size = STRIP_ROWS * lane_count
    per_replica = CROSS_MAX * width
    ids = picked_ids.reshape(REPLICAS, per_replica)
    dest = ids // strip_size
    inside = ids % strip_size
    order = jnp.arange(per_replica, dtype=jnp.int32)
    same = (dest[:, :, None] == dest[:, None, :]) & (order[None, None, :] < order[None, :, None])
    rank = jnp.sum(same.astype(jnp.int32), axis=2)
    slots = REPLICAS * blocks
    fields = jnp.concatenate(
        [
            jnp.transpose(values.reshape(3, REPLICAS, per_replica), (1, 2, 0)),
            (inside // lane_count).astype(jnp.bfloat16)[:, :, None],
            (inside % lane_count).astype(jnp.bfloat16)[:, :, None],
        ],
        axis=2,
    )
    dest_hits = (dest[:, :, None] == jnp.arange(devices, dtype=jnp.int32)).astype(jnp.bfloat16)
    rank_hits = (rank[:, :, None] == jnp.arange(blocks, dtype=jnp.int32)).astype(jnp.bfloat16)
    placed = (fields[:, :, :, None] * rank_hits[:, :, None, :]).reshape(REPLICAS, per_replica, 5 * blocks)
    send = lax.dot_general(
        dest_hits, placed, (((1,), (1,)), ((0,), (0,))), preferred_element_type=jnp.float32
    )
    send = jnp.transpose(send.reshape(REPLICAS, devices, 5, blocks), (1, 2, 0, 3))
    send = send.reshape(devices, 5, slots)
    pixel = send[:, 3] * lane_count + send[:, 4]
    half = lane_count // 2
    pad = ((0, 0), (0, half - slots))
    send = jnp.stack(
        [
            jnp.concatenate([jnp.pad(send[:, 0], pad), jnp.pad(send[:, 1], pad)], axis=1),
            jnp.concatenate([jnp.pad(send[:, 2], pad), jnp.pad(pixel, pad)], axis=1),
        ],
        axis=1,
    )
    got = exchange(send, count_y)
    got_values = [got[:, 0, :half], got[:, 0, half:], got[:, 1, :half]]
    got_pixel = got[:, 1, half:].astype(jnp.int32).reshape(1, devices * half)
    row_hits = (got_pixel // lane_count == jnp.arange(STRIP_ROWS, dtype=jnp.int32)[:, None]).astype(
        jnp.bfloat16
    )
    lane_hits = got_pixel % lane_count == jnp.arange(lane_count, dtype=jnp.int32)[:, None]
    spread = jnp.concatenate(
        [jnp.where(lane_hits, value.reshape(1, devices * half), 0.0) for value in got_values], axis=0
    ).astype(jnp.bfloat16)
    maps = lax.dot_general(
        row_hits, spread, (((1,), (1,)), ((), ())), preferred_element_type=jnp.float32
    )
    return (new_places.reshape(3, blocks * width), new_speeds.reshape(3, blocks * width), maps)


def solution(mesh):
    in_specs = (
        P(None, ("gx", "gy")),
        P(None, ("gx", "gy")),
        P(("gx", "gy"), None),
        P(("gx", "gy"), None),
        P(),
        P(None, ("gx", "gy")),
    )
    out_specs = (P(None, ("gx", "gy")), P(None, ("gx", "gy")), P(("gx", "gy"), None))
    return jax.shard_map(
        on_device, mesh=mesh, in_specs=in_specs, out_specs=out_specs, check_vma=False
    )
```

```python
import jax
import jax.numpy as jnp
from jax import lax
from jax.experimental import pallas as pl
from jax.experimental.pallas import tpu as pltpu
from jax.sharding import PartitionSpec as P

MOVERS = 2
CROSS_MAX = 5
REPLICAS = 3
STRIP_ROWS = 64


time_step = 0.05
lane_count = 128
MESH = pl.DeviceIdType.MESH


def exchange_kernel(send_ref, out_ref, middle, recv, send_sems, recv_sems):
    count_x, count_y = send_ref.shape[0], send_ref.shape[1]
    x = lax.axis_index("gx")
    y = lax.axis_index("gy")
    barrier = pltpu.get_barrier_semaphore()

    def greet_y(offset, carry):
        where = (x, lax.rem(y + offset, count_y))
        pl.semaphore_signal(barrier, 1, device_id=where, device_id_type=MESH)
        return carry

    def greet_x(offset, carry):
        where = (lax.rem(x + offset, count_x), y)
        pl.semaphore_signal(barrier, 1, device_id=where, device_id_type=MESH)
        return carry

    lax.fori_loop(1, count_y, greet_y, 0)
    lax.fori_loop(1, count_x, greet_x, 0)
    pl.semaphore_wait(barrier, count_x + count_y - 2)

    pltpu.make_async_copy(send_ref.at[:, y], middle.at[y], recv_sems.at[0]).start()

    def post_y(offset, carry):
        other = lax.rem(y + offset, count_y)
        pltpu.make_async_remote_copy(
            src_ref=send_ref.at[:, other],
            dst_ref=middle.at[y],
            send_sem=send_sems.at[0],
            recv_sem=recv_sems.at[0],
            device_id=(x, other),
            device_id_type=MESH,
        ).start()
        return carry

    lax.fori_loop(1, count_y, post_y, 0)
    pltpu.make_async_copy(middle, middle, recv_sems.at[0]).wait()

    pltpu.make_async_copy(middle.at[:, x], recv.at[x], recv_sems.at[1]).start()

    def post_x(offset, carry):
        other = lax.rem(x + offset, count_x)
        pltpu.make_async_remote_copy(
            src_ref=middle.at[:, other],
            dst_ref=recv.at[x],
            send_sem=send_sems.at[1],
            recv_sem=recv_sems.at[1],
            device_id=(other, y),
            device_id_type=MESH,
        ).start()
        return carry

    lax.fori_loop(1, count_x, post_x, 0)
    pltpu.make_async_copy(recv, recv, recv_sems.at[1]).wait()
    pltpu.make_async_copy(
        middle.at[pl.ds(0, count_y - 1)], middle.at[pl.ds(0, count_y - 1)], send_sems.at[0]
    ).wait()
    pltpu.make_async_copy(
        recv.at[pl.ds(0, count_x - 1)], recv.at[pl.ds(0, count_x - 1)], send_sems.at[1]
    ).wait()
    out_ref[...] = recv[...]


def exchange(send, count_x, count_y):
    devices = send.shape[0]
    grid = send.reshape(count_x, count_y, *send.shape[1:])
    middle = (count_y, count_x) + send.shape[1:]
    got = pl.pallas_call(
        exchange_kernel,
        out_shape=jax.ShapeDtypeStruct(grid.shape, jnp.float32),
        in_specs=[pl.BlockSpec(memory_space=pltpu.VMEM)],
        out_specs=pl.BlockSpec(memory_space=pltpu.VMEM),
        scratch_shapes=[
            pltpu.VMEM(middle, jnp.float32),
            pltpu.VMEM(grid.shape, jnp.float32),
            pltpu.SemaphoreType.DMA((2,)),
            pltpu.SemaphoreType.DMA((2,)),
        ],
        compiler_params=pltpu.CompilerParams(collective_id=0, has_side_effects=True),
    )(grid)
    return got.reshape(send.shape)
def passed_along(block, axis, distance):
    devices = range(lax.axis_size(axis))
    route = [((i - distance) % len(devices), i) for i in devices]
    return lax.ppermute(block, axis, route)


def sky_terms(shifted, speeds, live_mask):
    radius = jnp.sum(shifted * shifted, axis=1)
    weight = 1.0 / (1.0 + radius)
    radial = jnp.sum(speeds[None] * shifted, axis=1) / jnp.sqrt(1.0 + radius)
    energy = jnp.sum(speeds * speeds, axis=0) / 3.0
    return jnp.stack(
        [weight * live_mask, weight * radial * live_mask, weight * energy[None] * live_mask], axis=0
    ).astype(jnp.bfloat16)


def on_device(positions, velocities, block_order, flags, offsets, pixels):
    blocks = block_order.shape[1]
    width = positions.shape[1] // blocks
    places = positions.reshape(3, blocks, width)
    speeds = velocities.reshape(3, blocks, width)
    places = places + time_step * speeds
    ordering = block_order[0]
    places = jnp.take(places, ordering, axis=1)
    speeds = jnp.take(speeds, ordering, axis=1)

    def leaving(which_set, component, sign_step):
        first_block = which_set * MOVERS
        moved_pos = places[:, first_block : first_block + MOVERS].at[component].add(sign_step)
        return (moved_pos, speeds[:, first_block : first_block + MOVERS])

    def moved(which_set, component, sign_step, axis, distance):
        pos, vel = leaving(which_set, component, sign_step)
        got = passed_along(jnp.concatenate([pos, vel], axis=0), axis, distance)
        return got[:3], got[3:]

    arrived = (
        moved(0, 0, -1.0, "gx", 1),
        moved(1, 0, 1.0, "gx", -1),
        moved(2, 1, -1.0, "gy", 1),
        moved(3, 1, 1.0, "gy", -1),
    )
    new_places = jnp.concatenate(
        [places[:, 4 * MOVERS :]] + [received[0] for received in arrived], axis=1
    )
    new_speeds = jnp.concatenate(
        [speeds[:, 4 * MOVERS :]] + [received[1] for received in arrived], axis=1
    )
    count_x = lax.axis_size("gx")
    count_y = lax.axis_size("gy")
    devices = count_x * count_y
    cell_x = lax.axis_index("gx")
    cell_y = lax.axis_index("gy")
    flag_row = flags[0]
    ranking = (1 - flag_row) * blocks + jnp.arange(blocks, dtype=jnp.int32)
    chosen = jnp.argsort(ranking)[:CROSS_MAX]
    live_mask = jnp.take(flag_row, chosen).astype(jnp.float32).reshape(1, CROSS_MAX, 1)
    picked_pos = jnp.take(new_places, chosen, axis=1)
    picked_vel = jnp.take(new_speeds, chosen, axis=1)
    picked_ids = jnp.take(pixels.reshape(REPLICAS, blocks, width), chosen, axis=1)
    global_pos = jnp.stack(
        [
            (cell_x.astype(jnp.float32) + picked_pos[0]) / count_x,
            (cell_y.astype(jnp.float32) + picked_pos[1]) / count_y,
            picked_pos[2],
        ],
        axis=0,
    )
    shifted = global_pos[None] + offsets.astype(jnp.float32)[:, :, None, None]
    values = sky_terms(shifted, picked_vel, live_mask)

    strip_size = STRIP_ROWS * lane_count
    per_replica = CROSS_MAX * width
    ids = picked_ids.reshape(REPLICAS, per_replica)
    dest = ids // strip_size
    inside = ids % strip_size
    order = jnp.arange(per_replica, dtype=jnp.int32)
    same = (dest[:, :, None] == dest[:, None, :]) & (order[None, None, :] < order[None, :, None])
    rank = jnp.sum(same.astype(jnp.int32), axis=2)
    slots = REPLICAS * blocks
    fields = jnp.concatenate(
        [
            jnp.transpose(values.reshape(3, REPLICAS, per_replica), (1, 2, 0)),
            (inside // lane_count).astype(jnp.bfloat16)[:, :, None],
            (inside % lane_count).astype(jnp.bfloat16)[:, :, None],
        ],
        axis=2,
    )
    dest_hits = (dest[:, :, None] == jnp.arange(devices, dtype=jnp.int32)).astype(jnp.bfloat16)
    rank_hits = (rank[:, :, None] == jnp.arange(blocks, dtype=jnp.int32)).astype(jnp.bfloat16)
    placed = (fields[:, :, :, None] * rank_hits[:, :, None, :]).reshape(REPLICAS, per_replica, 5 * blocks)
    send = lax.dot_general(
        dest_hits, placed, (((1,), (1,)), ((0,), (0,))), preferred_element_type=jnp.float32
    )
    send = jnp.transpose(send.reshape(REPLICAS, devices, 5, blocks), (1, 2, 0, 3))
    send = send.reshape(devices, 5, slots)
    pixel = send[:, 3] * lane_count + send[:, 4]
    half = lane_count // 2
    pad = ((0, 0), (0, half - slots))
    send = jnp.stack(
        [
            jnp.concatenate([jnp.pad(send[:, 0], pad), jnp.pad(send[:, 1], pad)], axis=1),
            jnp.concatenate([jnp.pad(send[:, 2], pad), jnp.pad(pixel, pad)], axis=1),
        ],
        axis=1,
    )
    got = exchange(send, count_x, count_y)
    got_values = jnp.stack([got[:, 0, :half], got[:, 0, half:], got[:, 1, :half]], axis=1)
    got_values = got_values.reshape(devices, 3, half).transpose(0, 2, 1).reshape(devices * half, 3)
    got_pixel = got[:, 1, half:].reshape(devices * half).astype(jnp.int32)
    rows = got_pixel // lane_count
    lanes = got_pixel % lane_count
    row_hits = (rows[None, :] == jnp.arange(STRIP_ROWS, dtype=jnp.int32)[:, None]).astype(jnp.bfloat16)
    lane_hits = (lanes[:, None] == jnp.arange(lane_count, dtype=jnp.int32)[None, :]).astype(jnp.bfloat16)
    spread = (got_values.astype(jnp.bfloat16)[:, :, None] * lane_hits[:, None, :]).reshape(
        devices * half, 3 * lane_count
    )
    maps = jnp.dot(row_hits, spread, preferred_element_type=jnp.float32)
    return (new_places.reshape(3, blocks * width), new_speeds.reshape(3, blocks * width), maps)


def solution(mesh):
    in_specs = (
        P(None, ("gx", "gy")),
        P(None, ("gx", "gy")),
        P(("gx", "gy"), None),
        P(("gx", "gy"), None),
        P(),
        P(None, ("gx", "gy")),
    )
    out_specs = (P(None, ("gx", "gy")), P(None, ("gx", "gy")), P(("gx", "gy"), None))
    return jax.shard_map(
        on_device, mesh=mesh, in_specs=in_specs, out_specs=out_specs, check_vma=False
    )
```

```python
import jax
import jax.numpy as jnp
from jax import lax
from jax.experimental import pallas as pl
from jax.experimental.pallas import tpu as pltpu
from jax.sharding import PartitionSpec as P

MOVERS = 2
CROSS_MAX = 5
REPLICAS = 3
STRIP_ROWS = 64


time_step = 0.05
lane_count = 128
MESH = pl.DeviceIdType.MESH


def exchange_kernel(send_ref, out_ref, middle, recv, send_sems, recv_sems):
    count_x, count_y = send_ref.shape[0], send_ref.shape[1]
    x = lax.axis_index("gx")
    y = lax.axis_index("gy")
    barrier = pltpu.get_barrier_semaphore()

    def greet_y(offset, carry):
        where = (x, lax.rem(y + offset, count_y))
        pl.semaphore_signal(barrier, 1, device_id=where, device_id_type=MESH)
        return carry

    def greet_x(offset, carry):
        where = (lax.rem(x + offset, count_x), y)
        pl.semaphore_signal(barrier, 1, device_id=where, device_id_type=MESH)
        return carry

    lax.fori_loop(1, count_y, greet_y, 0)
    lax.fori_loop(1, count_x, greet_x, 0)
    pl.semaphore_wait(barrier, count_x + count_y - 2)

    pltpu.make_async_copy(send_ref.at[:, y], middle.at[y], recv_sems.at[0]).start()

    def post_y(offset, carry):
        other = lax.rem(y + offset, count_y)
        pltpu.make_async_remote_copy(
            src_ref=send_ref.at[:, other],
            dst_ref=middle.at[y],
            send_sem=send_sems.at[0],
            recv_sem=recv_sems.at[0],
            device_id=(x, other),
            device_id_type=MESH,
        ).start()
        return carry

    lax.fori_loop(1, count_y, post_y, 0)
    pltpu.make_async_copy(middle, middle, recv_sems.at[0]).wait()

    pltpu.make_async_copy(middle.at[:, x], recv.at[x], recv_sems.at[1]).start()

    def post_x(offset, carry):
        other = lax.rem(x + offset, count_x)
        pltpu.make_async_remote_copy(
            src_ref=middle.at[:, other],
            dst_ref=recv.at[x],
            send_sem=send_sems.at[1],
            recv_sem=recv_sems.at[1],
            device_id=(other, y),
            device_id_type=MESH,
        ).start()
        return carry

    lax.fori_loop(1, count_x, post_x, 0)
    pltpu.make_async_copy(recv, recv, recv_sems.at[1]).wait()
    pltpu.make_async_copy(
        middle.at[pl.ds(0, count_y - 1)], middle.at[pl.ds(0, count_y - 1)], send_sems.at[0]
    ).wait()
    pltpu.make_async_copy(
        recv.at[pl.ds(0, count_x - 1)], recv.at[pl.ds(0, count_x - 1)], send_sems.at[1]
    ).wait()
    out_ref[...] = recv[...]


def exchange(send, count_x, count_y):
    devices = send.shape[0]
    grid = send.reshape(count_x, count_y, *send.shape[1:])
    middle = (count_y, count_x) + send.shape[1:]
    got = pl.pallas_call(
        exchange_kernel,
        out_shape=jax.ShapeDtypeStruct(grid.shape, jnp.float32),
        in_specs=[pl.BlockSpec(memory_space=pltpu.VMEM)],
        out_specs=pl.BlockSpec(memory_space=pltpu.VMEM),
        scratch_shapes=[
            pltpu.VMEM(middle, jnp.float32),
            pltpu.VMEM(grid.shape, jnp.float32),
            pltpu.SemaphoreType.DMA((2,)),
            pltpu.SemaphoreType.DMA((2,)),
        ],
        compiler_params=pltpu.CompilerParams(collective_id=0, has_side_effects=True),
    )(grid)
    return got.reshape(send.shape)
def passed_along(block, axis, distance):
    devices = range(lax.axis_size(axis))
    route = [((i - distance) % len(devices), i) for i in devices]
    return lax.ppermute(block, axis, route)


def sky_terms(shifted, speeds, live_mask):
    radius = jnp.sum(shifted * shifted, axis=1)
    weight = 1.0 / (1.0 + radius)
    radial = jnp.sum(speeds[None] * shifted, axis=1) / jnp.sqrt(1.0 + radius)
    energy = jnp.sum(speeds * speeds, axis=0) / 3.0
    return jnp.stack(
        [weight * live_mask, weight * radial * live_mask, weight * energy[None] * live_mask], axis=0
    ).astype(jnp.bfloat16)


def pick(data, hits):
    chosen = jnp.where(hits[:, :, None], data[..., None, :, :], jnp.zeros((), data.dtype))
    return jnp.sum(chosen, axis=-2)


def on_device(positions, velocities, block_order, flags, offsets, pixels):
    blocks = block_order.shape[1]
    width = positions.shape[1] // blocks
    block_ids = jnp.arange(blocks, dtype=jnp.int32)
    order_hits = block_order[0][:, None] == block_ids[None, :]
    places = pick(positions.reshape(3, blocks, width) + time_step * velocities.reshape(3, blocks, width), order_hits)
    speeds = pick(velocities.reshape(3, blocks, width), order_hits)

    flag_row = flags[0]
    earlier = block_ids[None, :] <= block_ids[:, None]
    flagged_upto = jnp.sum(jnp.where(earlier, flag_row[None, :], 0), axis=1)
    flagged = jnp.sum(flag_row)
    place = jnp.where(flag_row == 1, flagged_upto - 1, flagged + block_ids - flagged_upto)
    chosen_hits = place[None, :] == jnp.arange(CROSS_MAX, dtype=jnp.int32)[:, None]
    live_mask = jnp.sum(jnp.where(chosen_hits, flag_row[None, :], 0), axis=1)
    live_mask = live_mask.astype(jnp.float32).reshape(1, CROSS_MAX, 1)
    picked_ids = pick(pixels.reshape(REPLICAS, blocks, width), chosen_hits)

    count_x = lax.axis_size("gx")
    count_y = lax.axis_size("gy")
    devices = count_x * count_y
    cell_x = lax.axis_index("gx")
    cell_y = lax.axis_index("gy")

    strip_size = STRIP_ROWS * lane_count
    per_replica = CROSS_MAX * width
    ids = picked_ids.reshape(REPLICAS, per_replica)
    dest = ids // strip_size
    inside = ids % strip_size
    order = jnp.arange(per_replica, dtype=jnp.int32)
    same = (dest[:, :, None] == dest[:, None, :]) & (order[None, None, :] < order[None, :, None])
    rank = jnp.sum(same.astype(jnp.int32), axis=2)
    dest_hits = (dest[:, :, None] == jnp.arange(devices, dtype=jnp.int32)).astype(jnp.bfloat16)
    rank_hits = (rank[:, :, None] == block_ids).astype(jnp.bfloat16)
    where_in_strip = jnp.stack(
        [(inside // lane_count).astype(jnp.bfloat16), (inside % lane_count).astype(jnp.bfloat16)], axis=2
    )

    def leaving(which_set, component, sign_step):
        first_block = which_set * MOVERS
        moved_pos = places[:, first_block : first_block + MOVERS].at[component].add(sign_step)
        return jnp.concatenate([moved_pos, speeds[:, first_block : first_block + MOVERS]], axis=0)

    outgoing = [leaving(0, 0, -1.0), leaving(1, 0, 1.0), leaving(2, 1, -1.0), leaving(3, 1, 1.0)]
    outgoing, places, speeds, dest_hits, rank_hits, where_in_strip, live_mask = lax.optimization_barrier(
        (outgoing, places, speeds, dest_hits, rank_hits, where_in_strip, live_mask)
    )
    routes = (("gx", 1), ("gx", -1), ("gy", 1), ("gy", -1))
    arrived = [passed_along(block, *route) for block, route in zip(outgoing, routes)]
    new_places = jnp.concatenate([places[:, 4 * MOVERS :]] + [got[:3] for got in arrived], axis=1)
    new_speeds = jnp.concatenate([speeds[:, 4 * MOVERS :]] + [got[3:] for got in arrived], axis=1)
    picked_pos = pick(new_places, chosen_hits)
    picked_vel = pick(new_speeds, chosen_hits)
    global_pos = jnp.stack(
        [
            (cell_x.astype(jnp.float32) + picked_pos[0]) / count_x,
            (cell_y.astype(jnp.float32) + picked_pos[1]) / count_y,
            picked_pos[2],
        ],
        axis=0,
    )
    shifted = global_pos[None] + offsets.astype(jnp.float32)[:, :, None, None]
    values = sky_terms(shifted, picked_vel, live_mask)

    slots = REPLICAS * blocks
    fields = jnp.concatenate(
        [jnp.transpose(values.reshape(3, REPLICAS, per_replica), (1, 2, 0)), where_in_strip], axis=2
    )
    placed = (fields[:, :, :, None] * rank_hits[:, :, None, :]).reshape(REPLICAS, per_replica, 5 * blocks)
    send = lax.dot_general(
        dest_hits, placed, (((1,), (1,)), ((0,), (0,))), preferred_element_type=jnp.float32
    )
    send = jnp.transpose(send.reshape(REPLICAS, devices, 5, blocks), (1, 2, 0, 3))
    send = send.reshape(devices, 5, slots)
    pixel = send[:, 3] * lane_count + send[:, 4]
    half = lane_count // 2
    pad = ((0, 0), (0, half - slots))
    send = jnp.stack(
        [
            jnp.concatenate([jnp.pad(send[:, 0], pad), jnp.pad(send[:, 1], pad)], axis=1),
            jnp.concatenate([jnp.pad(send[:, 2], pad), jnp.pad(pixel, pad)], axis=1),
        ],
        axis=1,
    )
    got = exchange(send, count_x, count_y)
    got_values = jnp.stack([got[:, 0, :half], got[:, 0, half:], got[:, 1, :half]], axis=1)
    got_values = got_values.reshape(devices, 3, half).transpose(0, 2, 1).reshape(devices * half, 3)
    got_pixel = got[:, 1, half:].reshape(devices * half).astype(jnp.int32)
    rows = got_pixel // lane_count
    lanes = got_pixel % lane_count
    row_hits = (rows[None, :] == jnp.arange(STRIP_ROWS, dtype=jnp.int32)[:, None]).astype(jnp.bfloat16)
    lane_hits = (lanes[:, None] == jnp.arange(lane_count, dtype=jnp.int32)[None, :]).astype(jnp.bfloat16)
    spread = (got_values.astype(jnp.bfloat16)[:, :, None] * lane_hits[:, None, :]).reshape(
        devices * half, 3 * lane_count
    )
    maps = jnp.dot(row_hits, spread, preferred_element_type=jnp.float32)
    return (new_places.reshape(3, blocks * width), new_speeds.reshape(3, blocks * width), maps)


def solution(mesh):
    in_specs = (
        P(None, ("gx", "gy")),
        P(None, ("gx", "gy")),
        P(("gx", "gy"), None),
        P(("gx", "gy"), None),
        P(),
        P(None, ("gx", "gy")),
    )
    out_specs = (P(None, ("gx", "gy")), P(None, ("gx", "gy")), P(("gx", "gy"), None))
    return jax.shard_map(
        on_device, mesh=mesh, in_specs=in_specs, out_specs=out_specs, check_vma=False
    )
```

```python
import jax
import jax.numpy as jnp
from jax import lax
from jax.experimental import pallas as pl
from jax.experimental.pallas import tpu as pltpu
from jax.sharding import PartitionSpec as P

MOVERS = 2
CROSS_MAX = 5
REPLICAS = 3
STRIP_ROWS = 64


time_step = 0.05
lane_count = 128
MESH = pl.DeviceIdType.MESH


def exchange_kernel(send_ref, out_ref, middle, recv, send_sems, recv_sems):
    count_x, count_y = send_ref.shape[0], send_ref.shape[1]
    x = lax.axis_index("gx")
    y = lax.axis_index("gy")
    barrier = pltpu.get_barrier_semaphore()

    def greet_y(offset, carry):
        where = (x, lax.rem(y + offset, count_y))
        pl.semaphore_signal(barrier, 1, device_id=where, device_id_type=MESH)
        return carry

    def greet_x(offset, carry):
        where = (lax.rem(x + offset, count_x), y)
        pl.semaphore_signal(barrier, 1, device_id=where, device_id_type=MESH)
        return carry

    lax.fori_loop(1, count_y, greet_y, 0)
    lax.fori_loop(1, count_x, greet_x, 0)
    pl.semaphore_wait(barrier, count_x + count_y - 2)

    pltpu.make_async_copy(send_ref.at[:, y], middle.at[y], recv_sems.at[0]).start()

    def post_y(offset, carry):
        other = lax.rem(y + offset, count_y)
        pltpu.make_async_remote_copy(
            src_ref=send_ref.at[:, other],
            dst_ref=middle.at[y],
            send_sem=send_sems.at[0],
            recv_sem=recv_sems.at[0],
            device_id=(x, other),
            device_id_type=MESH,
        ).start()
        return carry

    lax.fori_loop(1, count_y, post_y, 0)
    pltpu.make_async_copy(middle, middle, recv_sems.at[0]).wait()

    pltpu.make_async_copy(middle.at[:, x], recv.at[x], recv_sems.at[1]).start()

    def post_x(offset, carry):
        other = lax.rem(x + offset, count_x)
        pltpu.make_async_remote_copy(
            src_ref=middle.at[:, other],
            dst_ref=recv.at[x],
            send_sem=send_sems.at[1],
            recv_sem=recv_sems.at[1],
            device_id=(other, y),
            device_id_type=MESH,
        ).start()
        return carry

    lax.fori_loop(1, count_x, post_x, 0)
    pltpu.make_async_copy(recv, recv, recv_sems.at[1]).wait()
    pltpu.make_async_copy(
        middle.at[pl.ds(0, count_y - 1)], middle.at[pl.ds(0, count_y - 1)], send_sems.at[0]
    ).wait()
    pltpu.make_async_copy(
        recv.at[pl.ds(0, count_x - 1)], recv.at[pl.ds(0, count_x - 1)], send_sems.at[1]
    ).wait()
    out_ref[...] = recv[...]


def migrate_kernel(send_ref, out_ref, recv, send_sem, recv_sem):
    count_x = lax.axis_size("gx")
    count_y = lax.axis_size("gy")
    x = lax.axis_index("gx")
    y = lax.axis_index("gy")
    faces = (
        (lax.rem(x + 1, count_x), y),
        (lax.rem(x + count_x - 1, count_x), y),
        (x, lax.rem(y + 1, count_y)),
        (x, lax.rem(y + count_y - 1, count_y)),
    )
    barrier = pltpu.get_barrier_semaphore()
    for where in faces:
        pl.semaphore_signal(barrier, 1, device_id=where, device_id_type=MESH)
    pl.semaphore_wait(barrier, len(faces))
    copies = []
    for face, where in enumerate(faces):
        copy = pltpu.make_async_remote_copy(
            src_ref=send_ref.at[face],
            dst_ref=recv.at[face],
            send_sem=send_sem.at[face],
            recv_sem=recv_sem.at[face],
            device_id=where,
            device_id_type=MESH,
        )
        copy.start()
        copies.append(copy)
    for copy in copies:
        copy.wait()
    out_ref[...] = recv[...]


def migrate(leaving):
    faces = leaving.shape[0]
    return pl.pallas_call(
        migrate_kernel,
        out_shape=jax.ShapeDtypeStruct(leaving.shape, jnp.float32),
        in_specs=[pl.BlockSpec(memory_space=pltpu.VMEM)],
        out_specs=pl.BlockSpec(memory_space=pltpu.VMEM),
        scratch_shapes=[
            pltpu.VMEM(leaving.shape, jnp.float32),
            pltpu.SemaphoreType.DMA((faces,)),
            pltpu.SemaphoreType.DMA((faces,)),
        ],
        compiler_params=pltpu.CompilerParams(collective_id=1, has_side_effects=True),
    )(leaving)


def exchange(send, count_x, count_y):
    devices = send.shape[0]
    grid = send.reshape(count_x, count_y, *send.shape[1:])
    middle = (count_y, count_x) + send.shape[1:]
    got = pl.pallas_call(
        exchange_kernel,
        out_shape=jax.ShapeDtypeStruct(grid.shape, jnp.float32),
        in_specs=[pl.BlockSpec(memory_space=pltpu.VMEM)],
        out_specs=pl.BlockSpec(memory_space=pltpu.VMEM),
        scratch_shapes=[
            pltpu.VMEM(middle, jnp.float32),
            pltpu.VMEM(grid.shape, jnp.float32),
            pltpu.SemaphoreType.DMA((2,)),
            pltpu.SemaphoreType.DMA((2,)),
        ],
        compiler_params=pltpu.CompilerParams(collective_id=0, has_side_effects=True),
    )(grid)
    return got.reshape(send.shape)
def sky_terms(shifted, speeds, live_mask):
    radius = jnp.sum(shifted * shifted, axis=1)
    weight = 1.0 / (1.0 + radius)
    radial = jnp.sum(speeds[None] * shifted, axis=1) / jnp.sqrt(1.0 + radius)
    energy = jnp.sum(speeds * speeds, axis=0) / 3.0
    return jnp.stack(
        [weight * live_mask, weight * radial * live_mask, weight * energy[None] * live_mask], axis=0
    ).astype(jnp.bfloat16)


def pick(data, hits):
    chosen = jnp.where(hits[:, :, None], data[..., None, :, :], jnp.zeros((), data.dtype))
    return jnp.sum(chosen, axis=-2)


def on_device(positions, velocities, block_order, flags, offsets, pixels):
    blocks = block_order.shape[1]
    width = positions.shape[1] // blocks
    block_ids = jnp.arange(blocks, dtype=jnp.int32)
    order_hits = block_order[0][:, None] == block_ids[None, :]
    places = pick(positions.reshape(3, blocks, width) + time_step * velocities.reshape(3, blocks, width), order_hits)
    speeds = pick(velocities.reshape(3, blocks, width), order_hits)

    flag_row = flags[0]
    earlier = block_ids[None, :] <= block_ids[:, None]
    flagged_upto = jnp.sum(jnp.where(earlier, flag_row[None, :], 0), axis=1)
    flagged = jnp.sum(flag_row)
    place = jnp.where(flag_row == 1, flagged_upto - 1, flagged + block_ids - flagged_upto)
    chosen_hits = place[None, :] == jnp.arange(CROSS_MAX, dtype=jnp.int32)[:, None]
    live_mask = jnp.sum(jnp.where(chosen_hits, flag_row[None, :], 0), axis=1)
    live_mask = live_mask.astype(jnp.float32).reshape(1, CROSS_MAX, 1)
    picked_ids = pick(pixels.reshape(REPLICAS, blocks, width), chosen_hits)

    count_x = lax.axis_size("gx")
    count_y = lax.axis_size("gy")
    devices = count_x * count_y
    cell_x = lax.axis_index("gx")
    cell_y = lax.axis_index("gy")

    strip_size = STRIP_ROWS * lane_count
    per_replica = CROSS_MAX * width
    ids = picked_ids.reshape(REPLICAS, per_replica)
    dest = ids // strip_size
    inside = ids % strip_size
    order = jnp.arange(per_replica, dtype=jnp.int32)
    same = (dest[:, :, None] == dest[:, None, :]) & (order[None, None, :] < order[None, :, None])
    rank = jnp.sum(same.astype(jnp.int32), axis=2)
    dest_hits = (dest[:, :, None] == jnp.arange(devices, dtype=jnp.int32)).astype(jnp.bfloat16)
    rank_hits = (rank[:, :, None] == block_ids).astype(jnp.bfloat16)
    where_in_strip = jnp.stack(
        [(inside // lane_count).astype(jnp.bfloat16), (inside % lane_count).astype(jnp.bfloat16)], axis=2
    )

    def leaving(which_set, component, sign_step):
        first_block = which_set * MOVERS
        moved_pos = places[:, first_block : first_block + MOVERS].at[component].add(sign_step)
        return jnp.concatenate([moved_pos, speeds[:, first_block : first_block + MOVERS]], axis=0)

    outgoing = [leaving(0, 0, -1.0), leaving(1, 0, 1.0), leaving(2, 1, -1.0), leaving(3, 1, 1.0)]
    outgoing, places, speeds, dest_hits, rank_hits, where_in_strip, live_mask = lax.optimization_barrier(
        (outgoing, places, speeds, dest_hits, rank_hits, where_in_strip, live_mask)
    )
    arrived = migrate(jnp.stack(outgoing).reshape(4, 6, MOVERS * width)).reshape(4, 6, MOVERS, width)
    new_places = jnp.concatenate([places[:, 4 * MOVERS :]] + [got[:3] for got in arrived], axis=1)
    new_speeds = jnp.concatenate([speeds[:, 4 * MOVERS :]] + [got[3:] for got in arrived], axis=1)
    picked_pos = pick(new_places, chosen_hits)
    picked_vel = pick(new_speeds, chosen_hits)
    global_pos = jnp.stack(
        [
            (cell_x.astype(jnp.float32) + picked_pos[0]) / count_x,
            (cell_y.astype(jnp.float32) + picked_pos[1]) / count_y,
            picked_pos[2],
        ],
        axis=0,
    )
    shifted = global_pos[None] + offsets.astype(jnp.float32)[:, :, None, None]
    values = sky_terms(shifted, picked_vel, live_mask)

    slots = REPLICAS * blocks
    fields = jnp.concatenate(
        [jnp.transpose(values.reshape(3, REPLICAS, per_replica), (1, 2, 0)), where_in_strip], axis=2
    )
    placed = (fields[:, :, :, None] * rank_hits[:, :, None, :]).reshape(REPLICAS, per_replica, 5 * blocks)
    send = lax.dot_general(
        dest_hits, placed, (((1,), (1,)), ((0,), (0,))), preferred_element_type=jnp.float32
    )
    send = jnp.transpose(send.reshape(REPLICAS, devices, 5, blocks), (1, 2, 0, 3))
    send = send.reshape(devices, 5, slots)
    pixel = send[:, 3] * lane_count + send[:, 4]
    half = lane_count // 2
    pad = ((0, 0), (0, half - slots))
    send = jnp.stack(
        [
            jnp.concatenate([jnp.pad(send[:, 0], pad), jnp.pad(send[:, 1], pad)], axis=1),
            jnp.concatenate([jnp.pad(send[:, 2], pad), jnp.pad(pixel, pad)], axis=1),
        ],
        axis=1,
    )
    got = exchange(send, count_x, count_y)
    got_values = jnp.stack([got[:, 0, :half], got[:, 0, half:], got[:, 1, :half]], axis=1)
    got_values = got_values.reshape(devices, 3, half).transpose(0, 2, 1).reshape(devices * half, 3)
    got_pixel = got[:, 1, half:].reshape(devices * half).astype(jnp.int32)
    rows = got_pixel // lane_count
    lanes = got_pixel % lane_count
    row_hits = (rows[None, :] == jnp.arange(STRIP_ROWS, dtype=jnp.int32)[:, None]).astype(jnp.bfloat16)
    lane_hits = (lanes[:, None] == jnp.arange(lane_count, dtype=jnp.int32)[None, :]).astype(jnp.bfloat16)
    spread = (got_values.astype(jnp.bfloat16)[:, :, None] * lane_hits[:, None, :]).reshape(
        devices * half, 3 * lane_count
    )
    maps = jnp.dot(row_hits, spread, preferred_element_type=jnp.float32)
    return (new_places.reshape(3, blocks * width), new_speeds.reshape(3, blocks * width), maps)


def solution(mesh):
    in_specs = (
        P(None, ("gx", "gy")),
        P(None, ("gx", "gy")),
        P(("gx", "gy"), None),
        P(("gx", "gy"), None),
        P(),
        P(None, ("gx", "gy")),
    )
    out_specs = (P(None, ("gx", "gy")), P(None, ("gx", "gy")), P(("gx", "gy"), None))
    return jax.shard_map(
        on_device, mesh=mesh, in_specs=in_specs, out_specs=out_specs, check_vma=False
    )
```

```python
import jax
import jax.numpy as jnp
from jax import lax
from jax.experimental import pallas as pl
from jax.experimental.pallas import tpu as pltpu
from jax.sharding import PartitionSpec as P

MOVERS = 2
CROSS_MAX = 5
REPLICAS = 3
STRIP_ROWS = 64


time_step = 0.05
lane_count = 128
MESH = pl.DeviceIdType.MESH


def exchange_kernel(send_ref, out_ref, middle, recv, send_sems, recv_sems):
    count_x, count_y = send_ref.shape[0], send_ref.shape[1]
    x = lax.axis_index("gx")
    y = lax.axis_index("gy")
    barrier = pltpu.get_barrier_semaphore()

    def greet_y(offset, carry):
        where = (x, lax.rem(y + offset, count_y))
        pl.semaphore_signal(barrier, 1, device_id=where, device_id_type=MESH)
        return carry

    def greet_x(offset, carry):
        where = (lax.rem(x + offset, count_x), y)
        pl.semaphore_signal(barrier, 1, device_id=where, device_id_type=MESH)
        return carry

    lax.fori_loop(1, count_y, greet_y, 0)
    lax.fori_loop(1, count_x, greet_x, 0)
    pl.semaphore_wait(barrier, count_x + count_y - 2)

    pltpu.make_async_copy(send_ref.at[:, y], middle.at[y], recv_sems.at[0]).start()

    def post_y(offset, carry):
        other = lax.rem(y + offset, count_y)
        pltpu.make_async_remote_copy(
            src_ref=send_ref.at[:, other],
            dst_ref=middle.at[y],
            send_sem=send_sems.at[0],
            recv_sem=recv_sems.at[0],
            device_id=(x, other),
            device_id_type=MESH,
        ).start()
        return carry

    lax.fori_loop(1, count_y, post_y, 0)
    pltpu.make_async_copy(middle, middle, recv_sems.at[0]).wait()

    pltpu.make_async_copy(middle.at[:, x], recv.at[x], recv_sems.at[1]).start()

    def post_x(offset, carry):
        other = lax.rem(x + offset, count_x)
        pltpu.make_async_remote_copy(
            src_ref=middle.at[:, other],
            dst_ref=recv.at[x],
            send_sem=send_sems.at[1],
            recv_sem=recv_sems.at[1],
            device_id=(other, y),
            device_id_type=MESH,
        ).start()
        return carry

    lax.fori_loop(1, count_x, post_x, 0)
    pltpu.make_async_copy(recv, recv, recv_sems.at[1]).wait()
    pltpu.make_async_copy(
        middle.at[pl.ds(0, count_y - 1)], middle.at[pl.ds(0, count_y - 1)], send_sems.at[0]
    ).wait()
    pltpu.make_async_copy(
        recv.at[pl.ds(0, count_x - 1)], recv.at[pl.ds(0, count_x - 1)], send_sems.at[1]
    ).wait()
    for row in range(out_ref.shape[0]):
        out_ref[row] = recv[:, :, row, :]


def migrate_kernel(send_ref, out_ref, recv, send_sem, recv_sem):
    count_x = lax.axis_size("gx")
    count_y = lax.axis_size("gy")
    x = lax.axis_index("gx")
    y = lax.axis_index("gy")
    faces = (
        (lax.rem(x + 1, count_x), y),
        (lax.rem(x + count_x - 1, count_x), y),
        (x, lax.rem(y + 1, count_y)),
        (x, lax.rem(y + count_y - 1, count_y)),
    )
    barrier = pltpu.get_barrier_semaphore()
    for where in faces:
        pl.semaphore_signal(barrier, 1, device_id=where, device_id_type=MESH)
    pl.semaphore_wait(barrier, len(faces))
    copies = []
    for face, where in enumerate(faces):
        copy = pltpu.make_async_remote_copy(
            src_ref=send_ref.at[face],
            dst_ref=recv.at[face],
            send_sem=send_sem.at[face],
            recv_sem=recv_sem.at[face],
            device_id=where,
            device_id_type=MESH,
        )
        copy.start()
        copies.append(copy)
    for copy in copies:
        copy.wait()
    out_ref[...] = recv[...]


def migrate(leaving):
    faces = leaving.shape[0]
    return pl.pallas_call(
        migrate_kernel,
        out_shape=jax.ShapeDtypeStruct(leaving.shape, jnp.float32),
        in_specs=[pl.BlockSpec(memory_space=pltpu.VMEM)],
        out_specs=pl.BlockSpec(memory_space=pltpu.VMEM),
        scratch_shapes=[
            pltpu.VMEM(leaving.shape, jnp.float32),
            pltpu.SemaphoreType.DMA((faces,)),
            pltpu.SemaphoreType.DMA((faces,)),
        ],
        compiler_params=pltpu.CompilerParams(collective_id=1, has_side_effects=True),
    )(leaving)


def exchange(send, count_x, count_y):
    devices = send.shape[0]
    grid = send.reshape(count_x, count_y, *send.shape[1:])
    middle = (count_y, count_x) + send.shape[1:]
    got = pl.pallas_call(
        exchange_kernel,
        out_shape=jax.ShapeDtypeStruct((send.shape[1], count_x, count_y, send.shape[2]), jnp.float32),
        in_specs=[pl.BlockSpec(memory_space=pltpu.VMEM)],
        out_specs=pl.BlockSpec(memory_space=pltpu.VMEM),
        scratch_shapes=[
            pltpu.VMEM(middle, jnp.float32),
            pltpu.VMEM(grid.shape, jnp.float32),
            pltpu.SemaphoreType.DMA((2,)),
            pltpu.SemaphoreType.DMA((2,)),
        ],
        compiler_params=pltpu.CompilerParams(collective_id=0, has_side_effects=True),
    )(grid)
    return got.reshape(send.shape[1], devices, send.shape[2])
def sky_terms(shifted, speeds, live_mask):
    radius = jnp.sum(shifted * shifted, axis=1)
    weight = 1.0 / (1.0 + radius)
    radial = jnp.sum(speeds[None] * shifted, axis=1) / jnp.sqrt(1.0 + radius)
    energy = jnp.sum(speeds * speeds, axis=0) / 3.0
    return jnp.stack(
        [weight * live_mask, weight * radial * live_mask, weight * energy[None] * live_mask], axis=0
    ).astype(jnp.bfloat16)


def pick(data, hits):
    chosen = jnp.where(hits[:, :, None], data[..., None, :, :], jnp.zeros((), data.dtype))
    return jnp.sum(chosen, axis=-2)


def on_device(positions, velocities, block_order, flags, offsets, pixels):
    blocks = block_order.shape[1]
    width = positions.shape[1] // blocks
    block_ids = jnp.arange(blocks, dtype=jnp.int32)
    order_hits = block_order[0][:, None] == block_ids[None, :]
    places = pick(positions.reshape(3, blocks, width) + time_step * velocities.reshape(3, blocks, width), order_hits)
    speeds = pick(velocities.reshape(3, blocks, width), order_hits)

    flag_row = flags[0]
    earlier = block_ids[None, :] <= block_ids[:, None]
    flagged_upto = jnp.sum(jnp.where(earlier, flag_row[None, :], 0), axis=1)
    flagged = jnp.sum(flag_row)
    place = jnp.where(flag_row == 1, flagged_upto - 1, flagged + block_ids - flagged_upto)
    chosen_hits = place[None, :] == jnp.arange(CROSS_MAX, dtype=jnp.int32)[:, None]
    live_mask = jnp.sum(jnp.where(chosen_hits, flag_row[None, :], 0), axis=1)
    live_mask = live_mask.astype(jnp.float32).reshape(1, CROSS_MAX, 1)
    picked_ids = pick(pixels.reshape(REPLICAS, blocks, width), chosen_hits)

    count_x = lax.axis_size("gx")
    count_y = lax.axis_size("gy")
    devices = count_x * count_y
    cell_x = lax.axis_index("gx")
    cell_y = lax.axis_index("gy")

    strip_size = STRIP_ROWS * lane_count
    per_replica = CROSS_MAX * width
    ids = picked_ids.reshape(REPLICAS, per_replica)
    dest = ids // strip_size
    inside = ids % strip_size
    order = jnp.arange(per_replica, dtype=jnp.int32)
    same = (dest[:, :, None] == dest[:, None, :]) & (order[None, None, :] < order[None, :, None])
    rank = jnp.sum(same.astype(jnp.int32), axis=2)
    dest_hits = (dest[:, :, None] == jnp.arange(devices, dtype=jnp.int32)).astype(jnp.bfloat16)
    rank_hits = (rank[:, :, None] == block_ids).astype(jnp.bfloat16)
    where_in_strip = jnp.stack(
        [(inside // lane_count).astype(jnp.bfloat16), (inside % lane_count).astype(jnp.bfloat16)], axis=2
    )

    def leaving(which_set, component, sign_step):
        first_block = which_set * MOVERS
        moved_pos = places[:, first_block : first_block + MOVERS].at[component].add(sign_step)
        return jnp.concatenate([moved_pos, speeds[:, first_block : first_block + MOVERS]], axis=0)

    outgoing = [leaving(0, 0, -1.0), leaving(1, 0, 1.0), leaving(2, 1, -1.0), leaving(3, 1, 1.0)]
    outgoing, places, speeds, dest_hits, rank_hits, where_in_strip, live_mask = lax.optimization_barrier(
        (outgoing, places, speeds, dest_hits, rank_hits, where_in_strip, live_mask)
    )
    arrived = migrate(jnp.stack(outgoing).reshape(4, 6, MOVERS * width)).reshape(4, 6, MOVERS, width)
    new_places = jnp.concatenate([places[:, 4 * MOVERS :]] + [got[:3] for got in arrived], axis=1)
    new_speeds = jnp.concatenate([speeds[:, 4 * MOVERS :]] + [got[3:] for got in arrived], axis=1)
    picked_pos = pick(new_places, chosen_hits)
    picked_vel = pick(new_speeds, chosen_hits)
    global_pos = jnp.stack(
        [
            (cell_x.astype(jnp.float32) + picked_pos[0]) / count_x,
            (cell_y.astype(jnp.float32) + picked_pos[1]) / count_y,
            picked_pos[2],
        ],
        axis=0,
    )
    shifted = global_pos[None] + offsets.astype(jnp.float32)[:, :, None, None]
    values = sky_terms(shifted, picked_vel, live_mask)

    slots = REPLICAS * blocks
    fields = jnp.concatenate(
        [jnp.transpose(values.reshape(3, REPLICAS, per_replica), (1, 2, 0)), where_in_strip], axis=2
    )
    placed = (fields[:, :, :, None] * rank_hits[:, :, None, :]).reshape(REPLICAS, per_replica, 5 * blocks)
    send = lax.dot_general(
        dest_hits, placed, (((1,), (1,)), ((0,), (0,))), preferred_element_type=jnp.float32
    )
    send = jnp.transpose(send.reshape(REPLICAS, devices, 5, blocks), (1, 2, 0, 3))
    send = send.reshape(devices, 5, slots)
    pixel = send[:, 3] * lane_count + send[:, 4]
    half = lane_count // 2
    pad = ((0, 0), (0, half - slots))
    send = jnp.stack(
        [
            jnp.concatenate([jnp.pad(send[:, 0], pad), jnp.pad(send[:, 1], pad)], axis=1),
            jnp.concatenate([jnp.pad(send[:, 2], pad), jnp.pad(pixel, pad)], axis=1),
        ],
        axis=1,
    )
    got = exchange(send, count_x, count_y)
    got_values = jnp.stack([got[0, :, :half], got[0, :, half:], got[1, :, :half]], axis=1)
    got_values = got_values.reshape(devices, 3, half).transpose(0, 2, 1).reshape(devices * half, 3)
    got_pixel = got[1, :, half:].reshape(devices * half).astype(jnp.int32)
    rows = got_pixel // lane_count
    lanes = got_pixel % lane_count
    row_hits = (rows[None, :] == jnp.arange(STRIP_ROWS, dtype=jnp.int32)[:, None]).astype(jnp.bfloat16)
    lane_hits = (lanes[:, None] == jnp.arange(lane_count, dtype=jnp.int32)[None, :]).astype(jnp.bfloat16)
    spread = (got_values.astype(jnp.bfloat16)[:, :, None] * lane_hits[:, None, :]).reshape(
        devices * half, 3 * lane_count
    )
    maps = jnp.dot(row_hits, spread, preferred_element_type=jnp.float32)
    return (new_places.reshape(3, blocks * width), new_speeds.reshape(3, blocks * width), maps)


def solution(mesh):
    in_specs = (
        P(None, ("gx", "gy")),
        P(None, ("gx", "gy")),
        P(("gx", "gy"), None),
        P(("gx", "gy"), None),
        P(),
        P(None, ("gx", "gy")),
    )
    out_specs = (P(None, ("gx", "gy")), P(None, ("gx", "gy")), P(("gx", "gy"), None))
    return jax.shard_map(
        on_device, mesh=mesh, in_specs=in_specs, out_specs=out_specs, check_vma=False
    )
```

```python
import jax
import jax.numpy as jnp
from jax import lax
from jax.experimental import pallas as pl
from jax.experimental.pallas import tpu as pltpu
from jax.sharding import PartitionSpec as P

MOVERS = 2
CROSS_MAX = 5
REPLICAS = 3
STRIP_ROWS = 64


time_step = 0.05
lane_count = 128
MESH = pl.DeviceIdType.MESH


def exchange_kernel(send_ref, out_ref, middle, recv, send_sems, recv_sems):
    count_x, count_y = send_ref.shape[0], send_ref.shape[1]
    x = lax.axis_index("gx")
    y = lax.axis_index("gy")
    barrier = pltpu.get_barrier_semaphore()

    def greet_y(offset, carry):
        where = (x, lax.rem(y + offset, count_y))
        pl.semaphore_signal(barrier, 1, device_id=where, device_id_type=MESH)
        return carry

    def greet_x(offset, carry):
        where = (lax.rem(x + offset, count_x), y)
        pl.semaphore_signal(barrier, 1, device_id=where, device_id_type=MESH)
        return carry

    lax.fori_loop(1, count_y, greet_y, 0)
    lax.fori_loop(1, count_x, greet_x, 0)
    pl.semaphore_wait(barrier, count_x + count_y - 2)

    pltpu.make_async_copy(send_ref.at[:, y], middle.at[y], recv_sems.at[0]).start()

    def post_y(offset, carry):
        other = lax.rem(y + offset, count_y)
        pltpu.make_async_remote_copy(
            src_ref=send_ref.at[:, other],
            dst_ref=middle.at[y],
            send_sem=send_sems.at[0],
            recv_sem=recv_sems.at[0],
            device_id=(x, other),
            device_id_type=MESH,
        ).start()
        return carry

    lax.fori_loop(1, count_y, post_y, 0)
    pltpu.make_async_copy(middle, middle, recv_sems.at[0]).wait()

    pltpu.make_async_copy(middle.at[:, x], recv.at[x], recv_sems.at[1]).start()

    def post_x(offset, carry):
        other = lax.rem(x + offset, count_x)
        pltpu.make_async_remote_copy(
            src_ref=middle.at[:, other],
            dst_ref=recv.at[x],
            send_sem=send_sems.at[1],
            recv_sem=recv_sems.at[1],
            device_id=(other, y),
            device_id_type=MESH,
        ).start()
        return carry

    lax.fori_loop(1, count_x, post_x, 0)
    pltpu.make_async_copy(recv, recv, recv_sems.at[1]).wait()
    pltpu.make_async_copy(
        middle.at[pl.ds(0, count_y - 1)], middle.at[pl.ds(0, count_y - 1)], send_sems.at[0]
    ).wait()
    pltpu.make_async_copy(
        recv.at[pl.ds(0, count_x - 1)], recv.at[pl.ds(0, count_x - 1)], send_sems.at[1]
    ).wait()
    for row in range(out_ref.shape[0]):
        out_ref[row] = recv[:, :, row, :]


def migrate_kernel(send_ref, out_ref, recv, send_sem, recv_sem):
    count_x = lax.axis_size("gx")
    count_y = lax.axis_size("gy")
    x = lax.axis_index("gx")
    y = lax.axis_index("gy")
    faces = (
        (lax.rem(x + 1, count_x), y),
        (lax.rem(x + count_x - 1, count_x), y),
        (x, lax.rem(y + 1, count_y)),
        (x, lax.rem(y + count_y - 1, count_y)),
    )
    barrier = pltpu.get_barrier_semaphore()
    for where in faces:
        pl.semaphore_signal(barrier, 1, device_id=where, device_id_type=MESH)
    pl.semaphore_wait(barrier, len(faces))
    copies = []
    for face, where in enumerate(faces):
        copy = pltpu.make_async_remote_copy(
            src_ref=send_ref.at[face],
            dst_ref=recv.at[face],
            send_sem=send_sem.at[face],
            recv_sem=recv_sem.at[face],
            device_id=where,
            device_id_type=MESH,
        )
        copy.start()
        copies.append(copy)
    for copy in copies:
        copy.wait()
    out_ref[...] = recv[...]


def migrate(leaving):
    faces = leaving.shape[0]
    return pl.pallas_call(
        migrate_kernel,
        out_shape=jax.ShapeDtypeStruct(leaving.shape, jnp.float32),
        in_specs=[pl.BlockSpec(memory_space=pltpu.VMEM)],
        out_specs=pl.BlockSpec(memory_space=pltpu.VMEM),
        scratch_shapes=[
            pltpu.VMEM(leaving.shape, jnp.float32),
            pltpu.SemaphoreType.DMA((faces,)),
            pltpu.SemaphoreType.DMA((faces,)),
        ],
        compiler_params=pltpu.CompilerParams(collective_id=1, has_side_effects=True),
    )(leaving)


def exchange(send, count_x, count_y):
    devices = send.shape[0]
    grid = send.reshape(count_x, count_y, *send.shape[1:])
    middle = (count_y, count_x) + send.shape[1:]
    got = pl.pallas_call(
        exchange_kernel,
        out_shape=jax.ShapeDtypeStruct((send.shape[1], count_x, count_y, send.shape[2]), jnp.float32),
        in_specs=[pl.BlockSpec(memory_space=pltpu.VMEM)],
        out_specs=pl.BlockSpec(memory_space=pltpu.VMEM),
        scratch_shapes=[
            pltpu.VMEM(middle, jnp.float32),
            pltpu.VMEM(grid.shape, jnp.float32),
            pltpu.SemaphoreType.DMA((2,)),
            pltpu.SemaphoreType.DMA((2,)),
        ],
        compiler_params=pltpu.CompilerParams(collective_id=0, has_side_effects=True),
    )(grid)
    return got.reshape(send.shape[1], devices, send.shape[2])
def sky_terms(shifted, speeds, live_mask):
    radius = jnp.sum(shifted * shifted, axis=1)
    weight = 1.0 / (1.0 + radius)
    radial = jnp.sum(speeds[None] * shifted, axis=1) / jnp.sqrt(1.0 + radius)
    energy = jnp.sum(speeds * speeds, axis=0) / 3.0
    return jnp.stack(
        [weight * live_mask, weight * radial * live_mask, weight * energy[None] * live_mask], axis=0
    ).astype(jnp.bfloat16)


def pick(data, hits):
    chosen = jnp.where(hits[:, :, None], data[..., None, :, :], jnp.zeros((), data.dtype))
    return jnp.sum(chosen, axis=-2)


def on_device(positions, velocities, block_order, flags, offsets, pixels):
    blocks = block_order.shape[1]
    width = positions.shape[1] // blocks
    block_ids = jnp.arange(blocks, dtype=jnp.int32)
    order_hits = block_order[0][:, None] == block_ids[None, :]
    places = pick(positions.reshape(3, blocks, width) + time_step * velocities.reshape(3, blocks, width), order_hits)
    speeds = pick(velocities.reshape(3, blocks, width), order_hits)

    flag_row = flags[0]
    earlier = block_ids[None, :] <= block_ids[:, None]
    flagged_upto = jnp.sum(jnp.where(earlier, flag_row[None, :], 0), axis=1)
    flagged = jnp.sum(flag_row)
    place = jnp.where(flag_row == 1, flagged_upto - 1, flagged + block_ids - flagged_upto)
    chosen_hits = place[None, :] == jnp.arange(CROSS_MAX, dtype=jnp.int32)[:, None]
    live_mask = jnp.sum(jnp.where(chosen_hits, flag_row[None, :], 0), axis=1)
    live_mask = live_mask.astype(jnp.float32).reshape(1, CROSS_MAX, 1)
    picked_ids = pick(pixels.reshape(REPLICAS, blocks, width), chosen_hits)

    count_x = lax.axis_size("gx")
    count_y = lax.axis_size("gy")
    devices = count_x * count_y
    cell_x = lax.axis_index("gx")
    cell_y = lax.axis_index("gy")

    strip_size = STRIP_ROWS * lane_count
    per_replica = CROSS_MAX * width
    ids = picked_ids.reshape(REPLICAS, per_replica)
    dest = ids // strip_size
    inside = ids % strip_size
    order = jnp.arange(per_replica, dtype=jnp.int32)
    same = (dest[:, :, None] == dest[:, None, :]) & (order[None, None, :] < order[None, :, None])
    rank = jnp.sum(same.astype(jnp.int32), axis=2)
    dest_hits = (dest[:, :, None] == jnp.arange(devices, dtype=jnp.int32)).astype(jnp.bfloat16)
    rank_hits = (rank[:, :, None] == block_ids).astype(jnp.bfloat16)
    where_in_strip = jnp.stack(
        [(inside // lane_count).astype(jnp.bfloat16), (inside % lane_count).astype(jnp.bfloat16)], axis=2
    )

    def leaving(which_set, component, sign_step):
        first_block = which_set * MOVERS
        moved_pos = places[:, first_block : first_block + MOVERS].at[component].add(sign_step)
        return jnp.concatenate([moved_pos, speeds[:, first_block : first_block + MOVERS]], axis=0)

    outgoing = [leaving(0, 0, -1.0), leaving(1, 0, 1.0), leaving(2, 1, -1.0), leaving(3, 1, 1.0)]
    arrived = migrate(jnp.stack(outgoing).reshape(4, 6, MOVERS * width)).reshape(4, 6, MOVERS, width)
    new_places = jnp.concatenate([places[:, 4 * MOVERS :]] + [got[:3] for got in arrived], axis=1)
    new_speeds = jnp.concatenate([speeds[:, 4 * MOVERS :]] + [got[3:] for got in arrived], axis=1)
    picked_pos = pick(new_places, chosen_hits)
    picked_vel = pick(new_speeds, chosen_hits)
    global_pos = jnp.stack(
        [
            (cell_x.astype(jnp.float32) + picked_pos[0]) / count_x,
            (cell_y.astype(jnp.float32) + picked_pos[1]) / count_y,
            picked_pos[2],
        ],
        axis=0,
    )
    shifted = global_pos[None] + offsets.astype(jnp.float32)[:, :, None, None]
    values = sky_terms(shifted, picked_vel, live_mask)

    slots = REPLICAS * blocks
    fields = jnp.concatenate(
        [jnp.transpose(values.reshape(3, REPLICAS, per_replica), (1, 2, 0)), where_in_strip], axis=2
    )
    placed = (fields[:, :, :, None] * rank_hits[:, :, None, :]).reshape(REPLICAS, per_replica, 5 * blocks)
    send = lax.dot_general(
        dest_hits, placed, (((1,), (1,)), ((0,), (0,))), preferred_element_type=jnp.float32
    )
    send = jnp.transpose(send.reshape(REPLICAS, devices, 5, blocks), (1, 2, 0, 3))
    send = send.reshape(devices, 5, slots)
    pixel = send[:, 3] * lane_count + send[:, 4]
    half = lane_count // 2
    pad = ((0, 0), (0, half - slots))
    send = jnp.stack(
        [
            jnp.concatenate([jnp.pad(send[:, 0], pad), jnp.pad(send[:, 1], pad)], axis=1),
            jnp.concatenate([jnp.pad(send[:, 2], pad), jnp.pad(pixel, pad)], axis=1),
        ],
        axis=1,
    )
    got = exchange(send, count_x, count_y)
    got_values = jnp.stack([got[0, :, :half], got[0, :, half:], got[1, :, :half]], axis=1)
    got_values = got_values.reshape(devices, 3, half).transpose(0, 2, 1).reshape(devices * half, 3)
    got_pixel = got[1, :, half:].reshape(devices * half).astype(jnp.int32)
    rows = got_pixel // lane_count
    lanes = got_pixel % lane_count
    row_hits = (rows[None, :] == jnp.arange(STRIP_ROWS, dtype=jnp.int32)[:, None]).astype(jnp.bfloat16)
    lane_hits = (lanes[:, None] == jnp.arange(lane_count, dtype=jnp.int32)[None, :]).astype(jnp.bfloat16)
    spread = (got_values.astype(jnp.bfloat16)[:, :, None] * lane_hits[:, None, :]).reshape(
        devices * half, 3 * lane_count
    )
    maps = jnp.dot(row_hits, spread, preferred_element_type=jnp.float32)
    return (new_places.reshape(3, blocks * width), new_speeds.reshape(3, blocks * width), maps)


def solution(mesh):
    in_specs = (
        P(None, ("gx", "gy")),
        P(None, ("gx", "gy")),
        P(("gx", "gy"), None),
        P(("gx", "gy"), None),
        P(),
        P(None, ("gx", "gy")),
    )
    out_specs = (P(None, ("gx", "gy")), P(None, ("gx", "gy")), P(("gx", "gy"), None))
    return jax.shard_map(
        on_device, mesh=mesh, in_specs=in_specs, out_specs=out_specs, check_vma=False
    )
```

```python
import jax
import jax.numpy as jnp
from jax import lax
from jax.experimental import pallas as pl
from jax.experimental.pallas import tpu as pltpu
from jax.sharding import PartitionSpec as P

MOVERS = 2
CROSS_MAX = 5
REPLICAS = 3
STRIP_ROWS = 64


time_step = 0.05
lane_count = 128
MESH = pl.DeviceIdType.MESH


def exchange_kernel(send_ref, out_ref, middle, recv, send_sems, recv_sems):
    count_x, count_y = send_ref.shape[0], send_ref.shape[1]
    x = lax.axis_index("gx")
    y = lax.axis_index("gy")
    barrier = pltpu.get_barrier_semaphore()

    def greet_y(offset, carry):
        where = (x, lax.rem(y + offset, count_y))
        pl.semaphore_signal(barrier, 1, device_id=where, device_id_type=MESH)
        return carry

    def greet_x(offset, carry):
        where = (lax.rem(x + offset, count_x), y)
        pl.semaphore_signal(barrier, 1, device_id=where, device_id_type=MESH)
        return carry

    lax.fori_loop(1, count_y, greet_y, 0)
    lax.fori_loop(1, count_x, greet_x, 0)
    pl.semaphore_wait(barrier, count_x + count_y - 2)

    pltpu.make_async_copy(send_ref.at[:, y], middle.at[y], recv_sems.at[0]).start()

    def post_y(offset, carry):
        other = lax.rem(y + offset, count_y)
        pltpu.make_async_remote_copy(
            src_ref=send_ref.at[:, other],
            dst_ref=middle.at[y],
            send_sem=send_sems.at[0],
            recv_sem=recv_sems.at[0],
            device_id=(x, other),
            device_id_type=MESH,
        ).start()
        return carry

    lax.fori_loop(1, count_y, post_y, 0)
    pltpu.make_async_copy(middle, middle, recv_sems.at[0]).wait()

    pltpu.make_async_copy(middle.at[:, x], recv.at[x], recv_sems.at[1]).start()

    def post_x(offset, carry):
        other = lax.rem(x + offset, count_x)
        pltpu.make_async_remote_copy(
            src_ref=middle.at[:, other],
            dst_ref=recv.at[x],
            send_sem=send_sems.at[1],
            recv_sem=recv_sems.at[1],
            device_id=(other, y),
            device_id_type=MESH,
        ).start()
        return carry

    lax.fori_loop(1, count_x, post_x, 0)
    pltpu.make_async_copy(recv, recv, recv_sems.at[1]).wait()
    pltpu.make_async_copy(
        middle.at[pl.ds(0, count_y - 1)], middle.at[pl.ds(0, count_y - 1)], send_sems.at[0]
    ).wait()
    pltpu.make_async_copy(
        recv.at[pl.ds(0, count_x - 1)], recv.at[pl.ds(0, count_x - 1)], send_sems.at[1]
    ).wait()
    for row in range(out_ref.shape[0]):
        out_ref[row] = recv[:, :, row, :]


def migrate_kernel(send_ref, out_ref, recv, send_sem, recv_sem):
    count_x = lax.axis_size("gx")
    count_y = lax.axis_size("gy")
    x = lax.axis_index("gx")
    y = lax.axis_index("gy")
    faces = (
        (lax.rem(x + 1, count_x), y),
        (lax.rem(x + count_x - 1, count_x), y),
        (x, lax.rem(y + 1, count_y)),
        (x, lax.rem(y + count_y - 1, count_y)),
    )
    barrier = pltpu.get_barrier_semaphore()
    for where in faces:
        pl.semaphore_signal(barrier, 1, device_id=where, device_id_type=MESH)
    pl.semaphore_wait(barrier, len(faces))
    copies = []
    for face, where in enumerate(faces):
        copy = pltpu.make_async_remote_copy(
            src_ref=send_ref.at[face],
            dst_ref=recv.at[face],
            send_sem=send_sem.at[face],
            recv_sem=recv_sem.at[face],
            device_id=where,
            device_id_type=MESH,
        )
        copy.start()
        copies.append(copy)
    for copy in copies:
        copy.wait()
    out_ref[...] = recv[...]


def migrate(leaving):
    faces = leaving.shape[0]
    return pl.pallas_call(
        migrate_kernel,
        out_shape=jax.ShapeDtypeStruct(leaving.shape, jnp.float32),
        in_specs=[pl.BlockSpec(memory_space=pltpu.VMEM)],
        out_specs=pl.BlockSpec(memory_space=pltpu.VMEM),
        scratch_shapes=[
            pltpu.VMEM(leaving.shape, jnp.float32),
            pltpu.SemaphoreType.DMA((faces,)),
            pltpu.SemaphoreType.DMA((faces,)),
        ],
        compiler_params=pltpu.CompilerParams(collective_id=1, has_side_effects=True),
    )(leaving)


def bucket_kernel(flags_ref, offsets_ref, places_ref, speeds_ref, pixels_ref, send_ref):
    blocks = flags_ref.shape[1]
    devices = send_ref.shape[0]
    count_x = lax.axis_size("gx")
    count_y = lax.axis_size("gy")
    cell_x = lax.axis_index("gx").astype(jnp.float32)
    cell_y = lax.axis_index("gy").astype(jnp.float32)
    strip_size = STRIP_ROWS * lane_count
    half = lane_count // 2

    flag = [flags_ref[0, b] for b in range(blocks)]
    flagged = sum(flag)
    place, upto = [], 0
    for b in range(blocks):
        upto = upto + flag[b]
        place.append(jnp.where(flag[b] == 1, upto - 1, flagged + b - upto))
    chosen = [sum(jnp.where(place[b] == k, b, 0) for b in range(blocks)) for k in range(CROSS_MAX)]
    live = [sum(jnp.where(place[b] == k, flag[b], 0) for b in range(blocks)) for k in range(CROSS_MAX)]

    dest_iota = lax.broadcasted_iota(jnp.int32, (devices, lane_count), 0)
    slot_iota = lax.broadcasted_iota(jnp.int32, (lane_count, lane_count), 0)
    before = (
        lax.broadcasted_iota(jnp.int32, (lane_count, lane_count), 0)
        < lax.broadcasted_iota(jnp.int32, (lane_count, lane_count), 1)
    ).astype(jnp.bfloat16)
    nt = (((1,), (1,)), ((), ()))
    values_part = jnp.zeros((devices, lane_count), jnp.float32)
    strip_part = jnp.zeros((devices, lane_count), jnp.float32)
    lane_part = jnp.zeros((devices, lane_count), jnp.float32)
    for replica in range(REPLICAS):
        shift = [offsets_ref[replica, c].astype(jnp.float32) for c in range(3)]
        seen = jnp.zeros((devices, 1), jnp.float32)
        for k in range(CROSS_MAX):
            columns = pl.ds(pl.multiple_of(chosen[k] * lane_count, lane_count), lane_count)
            pos = places_ref[:, columns]
            vel = speeds_ref[:, columns]
            ids = pixels_ref[replica : replica + 1, columns]
            mask = live[k].astype(jnp.float32)
            s0 = (cell_x + pos[0:1]) / count_x + shift[0]
            s1 = (cell_y + pos[1:2]) / count_y + shift[1]
            s2 = pos[2:3] + shift[2]
            radius = s0 * s0 + s1 * s1 + s2 * s2
            weight = 1.0 / (1.0 + radius)
            radial = (vel[0:1] * s0 + vel[1:2] * s1 + vel[2:3] * s2) / jnp.sqrt(1.0 + radius)
            energy = (vel[0:1] * vel[0:1] + vel[1:2] * vel[1:2] + vel[2:3] * vel[2:3]) / 3.0
            value = [
                (weight * mask).astype(jnp.bfloat16).astype(jnp.float32),
                (weight * radial * mask).astype(jnp.bfloat16).astype(jnp.float32),
                (weight * energy * mask).astype(jnp.bfloat16).astype(jnp.float32),
            ]
            dest = ids // strip_size
            inside = ids % strip_size
            dest_hits = (dest == dest_iota).astype(jnp.bfloat16)
            counted = seen + jnp.dot(dest_hits, before, preferred_element_type=jnp.float32)
            rank = jnp.sum(dest_hits.astype(jnp.float32) * counted, axis=0, keepdims=True)
            seen = seen + jnp.sum(dest_hits.astype(jnp.float32), axis=1, keepdims=True)
            slot = rank.astype(jnp.int32) + replica * blocks
            low = slot_iota == slot
            high = slot_iota == slot + half
            first = (jnp.where(low, value[0], 0.0) + jnp.where(high, value[1], 0.0)).astype(jnp.bfloat16)
            second = jnp.where(low, value[2], 0.0) + jnp.where(high, (inside // lane_count).astype(jnp.float32), 0.0)
            third = jnp.where(high, (inside % lane_count).astype(jnp.float32), 0.0)
            values_part += lax.dot_general(dest_hits, first, nt, preferred_element_type=jnp.float32)
            strip_part += lax.dot_general(
                dest_hits, second.astype(jnp.bfloat16), nt, preferred_element_type=jnp.float32
            )
            lane_part += lax.dot_general(
                dest_hits, third.astype(jnp.bfloat16), nt, preferred_element_type=jnp.float32
            )
    scale = jnp.where(lax.broadcasted_iota(jnp.int32, (1, lane_count), 1) < half, 1.0, float(lane_count))
    send_ref[:, 0, :] = values_part
    send_ref[:, 1, :] = strip_part * scale + lane_part


def bucket(flags, offsets, places, speeds, pixels, devices):
    smem = pl.BlockSpec(memory_space=pltpu.SMEM)
    vmem = pl.BlockSpec(memory_space=pltpu.VMEM)
    return pl.pallas_call(
        bucket_kernel,
        out_shape=jax.ShapeDtypeStruct((devices, 2, lane_count), jnp.float32),
        in_specs=[smem, smem, vmem, vmem, vmem],
        out_specs=vmem,
    )(flags, offsets, places, speeds, pixels)


def exchange(send, count_x, count_y):
    devices = send.shape[0]
    grid = send.reshape(count_x, count_y, *send.shape[1:])
    middle = (count_y, count_x) + send.shape[1:]
    got = pl.pallas_call(
        exchange_kernel,
        out_shape=jax.ShapeDtypeStruct((send.shape[1], count_x, count_y, send.shape[2]), jnp.float32),
        in_specs=[pl.BlockSpec(memory_space=pltpu.VMEM)],
        out_specs=pl.BlockSpec(memory_space=pltpu.VMEM),
        scratch_shapes=[
            pltpu.VMEM(middle, jnp.float32),
            pltpu.VMEM(grid.shape, jnp.float32),
            pltpu.SemaphoreType.DMA((2,)),
            pltpu.SemaphoreType.DMA((2,)),
        ],
        compiler_params=pltpu.CompilerParams(collective_id=0, has_side_effects=True),
    )(grid)
    return got.reshape(send.shape[1], devices, send.shape[2])
def sky_terms(shifted, speeds, live_mask):
    radius = jnp.sum(shifted * shifted, axis=1)
    weight = 1.0 / (1.0 + radius)
    radial = jnp.sum(speeds[None] * shifted, axis=1) / jnp.sqrt(1.0 + radius)
    energy = jnp.sum(speeds * speeds, axis=0) / 3.0
    return jnp.stack(
        [weight * live_mask, weight * radial * live_mask, weight * energy[None] * live_mask], axis=0
    ).astype(jnp.bfloat16)


def pick(data, hits):
    chosen = jnp.where(hits[:, :, None], data[..., None, :, :], jnp.zeros((), data.dtype))
    return jnp.sum(chosen, axis=-2)


def on_device(positions, velocities, block_order, flags, offsets, pixels):
    blocks = block_order.shape[1]
    width = positions.shape[1] // blocks
    block_ids = jnp.arange(blocks, dtype=jnp.int32)
    order_hits = block_order[0][:, None] == block_ids[None, :]
    places = pick(positions.reshape(3, blocks, width) + time_step * velocities.reshape(3, blocks, width), order_hits)
    speeds = pick(velocities.reshape(3, blocks, width), order_hits)

    count_x = lax.axis_size("gx")
    count_y = lax.axis_size("gy")
    devices = count_x * count_y

    def leaving(which_set, component, sign_step):
        first_block = which_set * MOVERS
        moved_pos = places[:, first_block : first_block + MOVERS].at[component].add(sign_step)
        return jnp.concatenate([moved_pos, speeds[:, first_block : first_block + MOVERS]], axis=0)

    outgoing = [leaving(0, 0, -1.0), leaving(1, 0, 1.0), leaving(2, 1, -1.0), leaving(3, 1, 1.0)]
    arrived = migrate(jnp.stack(outgoing).reshape(4, 6, MOVERS * width)).reshape(4, 6, MOVERS, width)
    new_places = jnp.concatenate([places[:, 4 * MOVERS :]] + [got[:3] for got in arrived], axis=1)
    new_speeds = jnp.concatenate([speeds[:, 4 * MOVERS :]] + [got[3:] for got in arrived], axis=1)
    new_places = new_places.reshape(3, blocks * width)
    new_speeds = new_speeds.reshape(3, blocks * width)
    send = bucket(flags, offsets, new_places, new_speeds, pixels, devices)
    half = lane_count // 2
    got = exchange(send, count_x, count_y)
    got_values = jnp.stack([got[0, :, :half], got[0, :, half:], got[1, :, :half]], axis=1)
    got_values = got_values.reshape(devices, 3, half).transpose(0, 2, 1).reshape(devices * half, 3)
    got_pixel = got[1, :, half:].reshape(devices * half).astype(jnp.int32)
    rows = got_pixel // lane_count
    lanes = got_pixel % lane_count
    row_hits = (rows[None, :] == jnp.arange(STRIP_ROWS, dtype=jnp.int32)[:, None]).astype(jnp.bfloat16)
    lane_hits = (lanes[:, None] == jnp.arange(lane_count, dtype=jnp.int32)[None, :]).astype(jnp.bfloat16)
    spread = (got_values.astype(jnp.bfloat16)[:, :, None] * lane_hits[:, None, :]).reshape(
        devices * half, 3 * lane_count
    )
    maps = jnp.dot(row_hits, spread, preferred_element_type=jnp.float32)
    return (new_places, new_speeds, maps)


def solution(mesh):
    in_specs = (
        P(None, ("gx", "gy")),
        P(None, ("gx", "gy")),
        P(("gx", "gy"), None),
        P(("gx", "gy"), None),
        P(),
        P(None, ("gx", "gy")),
    )
    out_specs = (P(None, ("gx", "gy")), P(None, ("gx", "gy")), P(("gx", "gy"), None))
    return jax.shard_map(
        on_device, mesh=mesh, in_specs=in_specs, out_specs=out_specs, check_vma=False
    )
```

```python
import jax
import jax.numpy as jnp
from jax import lax
from jax.experimental import pallas as pl
from jax.experimental.pallas import tpu as pltpu
from jax.sharding import PartitionSpec as P

MOVERS = 2
CROSS_MAX = 5
REPLICAS = 3
STRIP_ROWS = 64


time_step = 0.05
lane_count = 128
MESH = pl.DeviceIdType.MESH


def exchange_kernel(flags_ref, offsets_ref, places_ref, speeds_ref, pixels_ref, out_ref, send_ref, middle, recv, send_sems, recv_sems):
    count_x, count_y = send_ref.shape[0], send_ref.shape[1]
    x = lax.axis_index("gx")
    y = lax.axis_index("gy")
    barrier = pltpu.get_barrier_semaphore()

    def greet_y(offset, carry):
        where = (x, lax.rem(y + offset, count_y))
        pl.semaphore_signal(barrier, 1, device_id=where, device_id_type=MESH)
        return carry

    def greet_x(offset, carry):
        where = (lax.rem(x + offset, count_x), y)
        pl.semaphore_signal(barrier, 1, device_id=where, device_id_type=MESH)
        return carry

    lax.fori_loop(1, count_y, greet_y, 0)
    lax.fori_loop(1, count_x, greet_x, 0)
    first, second = fill_send(flags_ref, offsets_ref, places_ref, speeds_ref, pixels_ref, count_x * count_y)
    for row in range(count_x):
        rows = slice(row * count_y, (row + 1) * count_y)
        send_ref[row, :, 0, :] = first[rows]
        send_ref[row, :, 1, :] = second[rows]
    pl.semaphore_wait(barrier, count_x + count_y - 2)

    pltpu.make_async_copy(send_ref.at[:, y], middle.at[y], recv_sems.at[0]).start()

    def post_y(offset, carry):
        other = lax.rem(y + offset, count_y)
        pltpu.make_async_remote_copy(
            src_ref=send_ref.at[:, other],
            dst_ref=middle.at[y],
            send_sem=send_sems.at[0],
            recv_sem=recv_sems.at[0],
            device_id=(x, other),
            device_id_type=MESH,
        ).start()
        return carry

    lax.fori_loop(1, count_y, post_y, 0)
    pltpu.make_async_copy(middle, middle, recv_sems.at[0]).wait()

    pltpu.make_async_copy(middle.at[:, x], recv.at[x], recv_sems.at[1]).start()

    def post_x(offset, carry):
        other = lax.rem(x + offset, count_x)
        pltpu.make_async_remote_copy(
            src_ref=middle.at[:, other],
            dst_ref=recv.at[x],
            send_sem=send_sems.at[1],
            recv_sem=recv_sems.at[1],
            device_id=(other, y),
            device_id_type=MESH,
        ).start()
        return carry

    lax.fori_loop(1, count_x, post_x, 0)
    pltpu.make_async_copy(recv, recv, recv_sems.at[1]).wait()
    pltpu.make_async_copy(
        middle.at[pl.ds(0, count_y - 1)], middle.at[pl.ds(0, count_y - 1)], send_sems.at[0]
    ).wait()
    pltpu.make_async_copy(
        recv.at[pl.ds(0, count_x - 1)], recv.at[pl.ds(0, count_x - 1)], send_sems.at[1]
    ).wait()
    for row in range(out_ref.shape[0]):
        out_ref[row] = recv[:, :, row, :]


def migrate_kernel(send_ref, out_ref, recv, send_sem, recv_sem):
    count_x = lax.axis_size("gx")
    count_y = lax.axis_size("gy")
    x = lax.axis_index("gx")
    y = lax.axis_index("gy")
    faces = (
        (lax.rem(x + 1, count_x), y),
        (lax.rem(x + count_x - 1, count_x), y),
        (x, lax.rem(y + 1, count_y)),
        (x, lax.rem(y + count_y - 1, count_y)),
    )
    barrier = pltpu.get_barrier_semaphore()
    for where in faces:
        pl.semaphore_signal(barrier, 1, device_id=where, device_id_type=MESH)
    pl.semaphore_wait(barrier, len(faces))
    copies = []
    for face, where in enumerate(faces):
        copy = pltpu.make_async_remote_copy(
            src_ref=send_ref.at[face],
            dst_ref=recv.at[face],
            send_sem=send_sem.at[face],
            recv_sem=recv_sem.at[face],
            device_id=where,
            device_id_type=MESH,
        )
        copy.start()
        copies.append(copy)
    for copy in copies:
        copy.wait()
    out_ref[...] = recv[...]


def migrate(leaving):
    faces = leaving.shape[0]
    return pl.pallas_call(
        migrate_kernel,
        out_shape=jax.ShapeDtypeStruct(leaving.shape, jnp.float32),
        in_specs=[pl.BlockSpec(memory_space=pltpu.VMEM)],
        out_specs=pl.BlockSpec(memory_space=pltpu.VMEM),
        scratch_shapes=[
            pltpu.VMEM(leaving.shape, jnp.float32),
            pltpu.SemaphoreType.DMA((faces,)),
            pltpu.SemaphoreType.DMA((faces,)),
        ],
        compiler_params=pltpu.CompilerParams(collective_id=1, has_side_effects=True),
    )(leaving)


def fill_send(flags_ref, offsets_ref, places_ref, speeds_ref, pixels_ref, devices):
    blocks = flags_ref.shape[1]
    count_x = lax.axis_size("gx")
    count_y = lax.axis_size("gy")
    cell_x = lax.axis_index("gx").astype(jnp.float32)
    cell_y = lax.axis_index("gy").astype(jnp.float32)
    strip_size = STRIP_ROWS * lane_count
    half = lane_count // 2

    flag = [flags_ref[0, b] for b in range(blocks)]
    flagged = sum(flag)
    place, upto = [], 0
    for b in range(blocks):
        upto = upto + flag[b]
        place.append(jnp.where(flag[b] == 1, upto - 1, flagged + b - upto))
    chosen = [sum(jnp.where(place[b] == k, b, 0) for b in range(blocks)) for k in range(CROSS_MAX)]
    live = [sum(jnp.where(place[b] == k, flag[b], 0) for b in range(blocks)) for k in range(CROSS_MAX)]

    def picked(ref, k):
        total = None
        for b in range(blocks):
            block = ref[:, b * lane_count : (b + 1) * lane_count]
            term = jnp.where(chosen[k] == b, block, jnp.zeros((), block.dtype))
            total = term if total is None else total + term
        return total

    picked_pos = [picked(places_ref, k) for k in range(CROSS_MAX)]
    picked_vel = [picked(speeds_ref, k) for k in range(CROSS_MAX)]
    picked_ids = [picked(pixels_ref, k) for k in range(CROSS_MAX)]
    dest_iota = lax.broadcasted_iota(jnp.int32, (devices, lane_count), 0)
    slot_iota = lax.broadcasted_iota(jnp.int32, (lane_count, lane_count), 0)
    before = (
        lax.broadcasted_iota(jnp.int32, (lane_count, lane_count), 0)
        < lax.broadcasted_iota(jnp.int32, (lane_count, lane_count), 1)
    ).astype(jnp.bfloat16)
    nt = (((1,), (1,)), ((), ()))
    values_part = jnp.zeros((devices, lane_count), jnp.float32)
    strip_part = jnp.zeros((devices, lane_count), jnp.float32)
    lane_part = jnp.zeros((devices, lane_count), jnp.float32)
    for replica in range(REPLICAS):
        shift = [offsets_ref[replica, c].astype(jnp.float32) for c in range(3)]
        seen = jnp.zeros((devices, 1), jnp.float32)
        for k in range(CROSS_MAX):
            pos, vel, ids = picked_pos[k], picked_vel[k], picked_ids[k][replica : replica + 1]
            mask = live[k].astype(jnp.float32)
            s0 = (cell_x + pos[0:1]) / count_x + shift[0]
            s1 = (cell_y + pos[1:2]) / count_y + shift[1]
            s2 = pos[2:3] + shift[2]
            radius = s0 * s0 + s1 * s1 + s2 * s2
            weight = 1.0 / (1.0 + radius)
            radial = (vel[0:1] * s0 + vel[1:2] * s1 + vel[2:3] * s2) / jnp.sqrt(1.0 + radius)
            energy = (vel[0:1] * vel[0:1] + vel[1:2] * vel[1:2] + vel[2:3] * vel[2:3]) / 3.0
            value = [
                (weight * mask).astype(jnp.bfloat16).astype(jnp.float32),
                (weight * radial * mask).astype(jnp.bfloat16).astype(jnp.float32),
                (weight * energy * mask).astype(jnp.bfloat16).astype(jnp.float32),
            ]
            dest = ids // strip_size
            inside = ids % strip_size
            dest_hits = (dest == dest_iota).astype(jnp.bfloat16)
            counted = seen + jnp.dot(dest_hits, before, preferred_element_type=jnp.float32)
            rank = jnp.sum(dest_hits.astype(jnp.float32) * counted, axis=0, keepdims=True)
            seen = seen + jnp.sum(dest_hits.astype(jnp.float32), axis=1, keepdims=True)
            slot = rank.astype(jnp.int32) + replica * blocks
            low = slot_iota == slot
            high = slot_iota == slot + half
            first = (jnp.where(low, value[0], 0.0) + jnp.where(high, value[1], 0.0)).astype(jnp.bfloat16)
            second = jnp.where(low, value[2], 0.0) + jnp.where(high, (inside // lane_count).astype(jnp.float32), 0.0)
            third = jnp.where(high, (inside % lane_count).astype(jnp.float32), 0.0)
            values_part += lax.dot_general(dest_hits, first, nt, preferred_element_type=jnp.float32)
            strip_part += lax.dot_general(
                dest_hits, second.astype(jnp.bfloat16), nt, preferred_element_type=jnp.float32
            )
            lane_part += lax.dot_general(
                dest_hits, third.astype(jnp.bfloat16), nt, preferred_element_type=jnp.float32
            )
    scale = jnp.where(lax.broadcasted_iota(jnp.int32, (1, lane_count), 1) < half, 1.0, float(lane_count))
    return values_part, strip_part * scale + lane_part


def exchange(flags, offsets, places, speeds, pixels, count_x, count_y):
    devices = count_x * count_y
    grid = (count_x, count_y, 2, lane_count)
    middle = (count_y, count_x, 2, lane_count)
    smem = pl.BlockSpec(memory_space=pltpu.SMEM)
    vmem = pl.BlockSpec(memory_space=pltpu.VMEM)
    got = pl.pallas_call(
        exchange_kernel,
        out_shape=jax.ShapeDtypeStruct((2, count_x, count_y, lane_count), jnp.float32),
        in_specs=[smem, smem, vmem, vmem, vmem],
        out_specs=vmem,
        scratch_shapes=[
            pltpu.VMEM(grid, jnp.float32),
            pltpu.VMEM(middle, jnp.float32),
            pltpu.VMEM(grid, jnp.float32),
            pltpu.SemaphoreType.DMA((2,)),
            pltpu.SemaphoreType.DMA((2,)),
        ],
        compiler_params=pltpu.CompilerParams(collective_id=0, has_side_effects=True),
    )(flags, offsets, places, speeds, pixels)
    return got.reshape(2, devices, lane_count)


def pick(data, hits):
    chosen = jnp.where(hits[:, :, None], data[..., None, :, :], jnp.zeros((), data.dtype))
    return jnp.sum(chosen, axis=-2)


def on_device(positions, velocities, block_order, flags, offsets, pixels):
    blocks = block_order.shape[1]
    width = positions.shape[1] // blocks
    block_ids = jnp.arange(blocks, dtype=jnp.int32)
    order_hits = block_order[0][:, None] == block_ids[None, :]
    places = pick(positions.reshape(3, blocks, width) + time_step * velocities.reshape(3, blocks, width), order_hits)
    speeds = pick(velocities.reshape(3, blocks, width), order_hits)

    count_x = lax.axis_size("gx")
    count_y = lax.axis_size("gy")
    devices = count_x * count_y

    def leaving(which_set, component, sign_step):
        first_block = which_set * MOVERS
        moved_pos = places[:, first_block : first_block + MOVERS].at[component].add(sign_step)
        return jnp.concatenate([moved_pos, speeds[:, first_block : first_block + MOVERS]], axis=0)

    outgoing = [leaving(0, 0, -1.0), leaving(1, 0, 1.0), leaving(2, 1, -1.0), leaving(3, 1, 1.0)]
    arrived = migrate(jnp.stack(outgoing).reshape(4, 6, MOVERS * width)).reshape(4, 6, MOVERS, width)
    new_places = jnp.concatenate([places[:, 4 * MOVERS :]] + [got[:3] for got in arrived], axis=1)
    new_speeds = jnp.concatenate([speeds[:, 4 * MOVERS :]] + [got[3:] for got in arrived], axis=1)
    new_places = new_places.reshape(3, blocks * width)
    new_speeds = new_speeds.reshape(3, blocks * width)
    half = lane_count // 2
    got = exchange(flags, offsets, new_places, new_speeds, pixels, count_x, count_y)
    got_values = jnp.stack([got[0, :, :half], got[0, :, half:], got[1, :, :half]], axis=1)
    got_values = got_values.reshape(devices, 3, half).transpose(0, 2, 1).reshape(devices * half, 3)
    got_pixel = got[1, :, half:].reshape(devices * half).astype(jnp.int32)
    rows = got_pixel // lane_count
    lanes = got_pixel % lane_count
    row_hits = (rows[None, :] == jnp.arange(STRIP_ROWS, dtype=jnp.int32)[:, None]).astype(jnp.bfloat16)
    lane_hits = (lanes[:, None] == jnp.arange(lane_count, dtype=jnp.int32)[None, :]).astype(jnp.bfloat16)
    spread = (got_values.astype(jnp.bfloat16)[:, :, None] * lane_hits[:, None, :]).reshape(
        devices * half, 3 * lane_count
    )
    maps = jnp.dot(row_hits, spread, preferred_element_type=jnp.float32)
    return (new_places, new_speeds, maps)


def solution(mesh):
    in_specs = (
        P(None, ("gx", "gy")),
        P(None, ("gx", "gy")),
        P(("gx", "gy"), None),
        P(("gx", "gy"), None),
        P(),
        P(None, ("gx", "gy")),
    )
    out_specs = (P(None, ("gx", "gy")), P(None, ("gx", "gy")), P(("gx", "gy"), None))
    return jax.shard_map(
        on_device, mesh=mesh, in_specs=in_specs, out_specs=out_specs, check_vma=False
    )
```

```python
import jax
import jax.numpy as jnp
from jax import lax
from jax.experimental import pallas as pl
from jax.experimental.pallas import tpu as pltpu
from jax.sharding import PartitionSpec as P

MOVERS = 2
CROSS_MAX = 5
REPLICAS = 3
STRIP_ROWS = 64


time_step = 0.05
lane_count = 128
MESH = pl.DeviceIdType.MESH


def exchange_kernel(flags_ref, offsets_ref, places_ref, speeds_ref, pixels_ref, out_ref, send_ref, middle, recv, send_sems, recv_sems):
    count_x, count_y = send_ref.shape[0], send_ref.shape[1]
    x = lax.axis_index("gx")
    y = lax.axis_index("gy")
    barrier = pltpu.get_barrier_semaphore()

    def greet_y(offset, carry):
        where = (x, lax.rem(y + offset, count_y))
        pl.semaphore_signal(barrier, 1, device_id=where, device_id_type=MESH)
        return carry

    def greet_x(offset, carry):
        where = (lax.rem(x + offset, count_x), y)
        pl.semaphore_signal(barrier, 1, device_id=where, device_id_type=MESH)
        return carry

    lax.fori_loop(1, count_y, greet_y, 0)
    lax.fori_loop(1, count_x, greet_x, 0)
    first, second = fill_send(flags_ref, offsets_ref, places_ref, speeds_ref, pixels_ref, count_x * count_y)
    for row in range(count_x):
        rows = slice(row * count_y, (row + 1) * count_y)
        send_ref[row, :, 0, :] = first[rows]
        send_ref[row, :, 1, :] = second[rows]
    pl.semaphore_wait(barrier, count_x + count_y - 2)

    pltpu.make_async_copy(send_ref.at[:, y], middle.at[y], recv_sems.at[0]).start()

    def post_y(offset, carry):
        other = lax.rem(y + offset, count_y)
        pltpu.make_async_remote_copy(
            src_ref=send_ref.at[:, other],
            dst_ref=middle.at[y],
            send_sem=send_sems.at[0],
            recv_sem=recv_sems.at[0],
            device_id=(x, other),
            device_id_type=MESH,
        ).start()
        return carry

    lax.fori_loop(1, count_y, post_y, 0)
    pltpu.make_async_copy(middle, middle, recv_sems.at[0]).wait()

    pltpu.make_async_copy(middle.at[:, x], recv.at[x], recv_sems.at[1]).start()

    def post_x(offset, carry):
        other = lax.rem(x + offset, count_x)
        pltpu.make_async_remote_copy(
            src_ref=middle.at[:, other],
            dst_ref=recv.at[x],
            send_sem=send_sems.at[1],
            recv_sem=recv_sems.at[1],
            device_id=(other, y),
            device_id_type=MESH,
        ).start()
        return carry

    lax.fori_loop(1, count_x, post_x, 0)
    pltpu.make_async_copy(recv, recv, recv_sems.at[1]).wait()
    pltpu.make_async_copy(
        middle.at[pl.ds(0, count_y - 1)], middle.at[pl.ds(0, count_y - 1)], send_sems.at[0]
    ).wait()
    pltpu.make_async_copy(
        recv.at[pl.ds(0, count_x - 1)], recv.at[pl.ds(0, count_x - 1)], send_sems.at[1]
    ).wait()
    for row in range(out_ref.shape[0]):
        out_ref[row] = recv[:, :, row, :]


def migrate_kernel(order_ref, positions_ref, velocities_ref, places_ref, speeds_ref, outgoing, recv, send_sem, recv_sem):
    count_x = lax.axis_size("gx")
    count_y = lax.axis_size("gy")
    x = lax.axis_index("gx")
    y = lax.axis_index("gy")
    faces = (
        (lax.rem(x + 1, count_x), y),
        (lax.rem(x + count_x - 1, count_x), y),
        (x, lax.rem(y + 1, count_y)),
        (x, lax.rem(y + count_y - 1, count_y)),
    )
    barrier = pltpu.get_barrier_semaphore()
    for where in faces:
        pl.semaphore_signal(barrier, 1, device_id=where, device_id_type=MESH)

    blocks = order_ref.shape[1]
    width = lane_count
    lanes = lambda b: slice(b * width, (b + 1) * width)
    drifted = [positions_ref[:, lanes(b)] + time_step * velocities_ref[:, lanes(b)] for b in range(blocks)]
    moving = [velocities_ref[:, lanes(b)] for b in range(blocks)]

    def ordered(source, k):
        total = None
        for b in range(blocks):
            term = jnp.where(order_ref[0, k] == b, source[b], 0.0)
            total = term if total is None else total + term
        return total

    stay = 4 * MOVERS
    for k in range(stay, blocks):
        places_ref[:, lanes(k - stay)] = ordered(drifted, k)
        speeds_ref[:, lanes(k - stay)] = ordered(moving, k)
    component_row = lax.broadcasted_iota(jnp.int32, (3, width), 0)
    steps = ((0, -1.0), (0, 1.0), (1, -1.0), (1, 1.0))
    for face, (component, sign_step) in enumerate(steps):
        for j in range(MOVERS):
            k = face * MOVERS + j
            moved = ordered(drifted, k) + jnp.where(component_row == component, sign_step, 0.0)
            outgoing[face, 0:3, lanes(j)] = moved
            outgoing[face, 3:6, lanes(j)] = ordered(moving, k)
    pl.semaphore_wait(barrier, len(faces))

    copies = []
    for face, where in enumerate(faces):
        copy = pltpu.make_async_remote_copy(
            src_ref=outgoing.at[face],
            dst_ref=recv.at[face],
            send_sem=send_sem.at[face],
            recv_sem=recv_sem.at[face],
            device_id=where,
            device_id_type=MESH,
        )
        copy.start()
        copies.append(copy)
    for copy in copies:
        copy.wait()
    for face in range(len(faces)):
        for j in range(MOVERS):
            k = blocks - stay + face * MOVERS + j
            places_ref[:, lanes(k)] = recv[face, 0:3, lanes(j)]
            speeds_ref[:, lanes(k)] = recv[face, 3:6, lanes(j)]


def migrate(block_order, positions, velocities):
    smem = pl.BlockSpec(memory_space=pltpu.SMEM)
    vmem = pl.BlockSpec(memory_space=pltpu.VMEM)
    buffer = (4, 6, MOVERS * lane_count)
    return pl.pallas_call(
        migrate_kernel,
        out_shape=(
            jax.ShapeDtypeStruct(positions.shape, jnp.float32),
            jax.ShapeDtypeStruct(velocities.shape, jnp.float32),
        ),
        in_specs=[smem, vmem, vmem],
        out_specs=(vmem, vmem),
        scratch_shapes=[
            pltpu.VMEM(buffer, jnp.float32),
            pltpu.VMEM(buffer, jnp.float32),
            pltpu.SemaphoreType.DMA((4,)),
            pltpu.SemaphoreType.DMA((4,)),
        ],
        compiler_params=pltpu.CompilerParams(collective_id=1, has_side_effects=True),
    )(block_order, positions, velocities)


def fill_send(flags_ref, offsets_ref, places_ref, speeds_ref, pixels_ref, devices):
    blocks = flags_ref.shape[1]
    count_x = lax.axis_size("gx")
    count_y = lax.axis_size("gy")
    cell_x = lax.axis_index("gx").astype(jnp.float32)
    cell_y = lax.axis_index("gy").astype(jnp.float32)
    strip_size = STRIP_ROWS * lane_count
    half = lane_count // 2

    flag = [flags_ref[0, b] for b in range(blocks)]
    flagged = sum(flag)
    place, upto = [], 0
    for b in range(blocks):
        upto = upto + flag[b]
        place.append(jnp.where(flag[b] == 1, upto - 1, flagged + b - upto))
    chosen = [sum(jnp.where(place[b] == k, b, 0) for b in range(blocks)) for k in range(CROSS_MAX)]
    live = [sum(jnp.where(place[b] == k, flag[b], 0) for b in range(blocks)) for k in range(CROSS_MAX)]

    def picked(ref, k):
        total = None
        for b in range(blocks):
            block = ref[:, b * lane_count : (b + 1) * lane_count]
            term = jnp.where(chosen[k] == b, block, jnp.zeros((), block.dtype))
            total = term if total is None else total + term
        return total

    picked_pos = [picked(places_ref, k) for k in range(CROSS_MAX)]
    picked_vel = [picked(speeds_ref, k) for k in range(CROSS_MAX)]
    picked_ids = [picked(pixels_ref, k) for k in range(CROSS_MAX)]
    dest_iota = lax.broadcasted_iota(jnp.int32, (devices, lane_count), 0)
    slot_iota = lax.broadcasted_iota(jnp.int32, (lane_count, lane_count), 0)
    before = (
        lax.broadcasted_iota(jnp.int32, (lane_count, lane_count), 0)
        < lax.broadcasted_iota(jnp.int32, (lane_count, lane_count), 1)
    ).astype(jnp.bfloat16)
    nt = (((1,), (1,)), ((), ()))
    values_part = jnp.zeros((devices, lane_count), jnp.float32)
    strip_part = jnp.zeros((devices, lane_count), jnp.float32)
    lane_part = jnp.zeros((devices, lane_count), jnp.float32)
    for replica in range(REPLICAS):
        shift = [offsets_ref[replica, c].astype(jnp.float32) for c in range(3)]
        seen = jnp.zeros((devices, 1), jnp.float32)
        for k in range(CROSS_MAX):
            pos, vel, ids = picked_pos[k], picked_vel[k], picked_ids[k][replica : replica + 1]
            mask = live[k].astype(jnp.float32)
            s0 = (cell_x + pos[0:1]) / count_x + shift[0]
            s1 = (cell_y + pos[1:2]) / count_y + shift[1]
            s2 = pos[2:3] + shift[2]
            radius = s0 * s0 + s1 * s1 + s2 * s2
            weight = 1.0 / (1.0 + radius)
            radial = (vel[0:1] * s0 + vel[1:2] * s1 + vel[2:3] * s2) / jnp.sqrt(1.0 + radius)
            energy = (vel[0:1] * vel[0:1] + vel[1:2] * vel[1:2] + vel[2:3] * vel[2:3]) / 3.0
            value = [
                (weight * mask).astype(jnp.bfloat16).astype(jnp.float32),
                (weight * radial * mask).astype(jnp.bfloat16).astype(jnp.float32),
                (weight * energy * mask).astype(jnp.bfloat16).astype(jnp.float32),
            ]
            dest = ids // strip_size
            inside = ids % strip_size
            dest_hits = (dest == dest_iota).astype(jnp.bfloat16)
            counted = seen + jnp.dot(dest_hits, before, preferred_element_type=jnp.float32)
            rank = jnp.sum(dest_hits.astype(jnp.float32) * counted, axis=0, keepdims=True)
            seen = seen + jnp.sum(dest_hits.astype(jnp.float32), axis=1, keepdims=True)
            slot = rank.astype(jnp.int32) + replica * blocks
            low = slot_iota == slot
            high = slot_iota == slot + half
            first = (jnp.where(low, value[0], 0.0) + jnp.where(high, value[1], 0.0)).astype(jnp.bfloat16)
            second = jnp.where(low, value[2], 0.0) + jnp.where(high, (inside // lane_count).astype(jnp.float32), 0.0)
            third = jnp.where(high, (inside % lane_count).astype(jnp.float32), 0.0)
            values_part += lax.dot_general(dest_hits, first, nt, preferred_element_type=jnp.float32)
            strip_part += lax.dot_general(
                dest_hits, second.astype(jnp.bfloat16), nt, preferred_element_type=jnp.float32
            )
            lane_part += lax.dot_general(
                dest_hits, third.astype(jnp.bfloat16), nt, preferred_element_type=jnp.float32
            )
    scale = jnp.where(lax.broadcasted_iota(jnp.int32, (1, lane_count), 1) < half, 1.0, float(lane_count))
    return values_part, strip_part * scale + lane_part


def exchange(flags, offsets, places, speeds, pixels, count_x, count_y):
    devices = count_x * count_y
    grid = (count_x, count_y, 2, lane_count)
    middle = (count_y, count_x, 2, lane_count)
    smem = pl.BlockSpec(memory_space=pltpu.SMEM)
    vmem = pl.BlockSpec(memory_space=pltpu.VMEM)
    got = pl.pallas_call(
        exchange_kernel,
        out_shape=jax.ShapeDtypeStruct((2, count_x, count_y, lane_count), jnp.float32),
        in_specs=[smem, smem, vmem, vmem, vmem],
        out_specs=vmem,
        scratch_shapes=[
            pltpu.VMEM(grid, jnp.float32),
            pltpu.VMEM(middle, jnp.float32),
            pltpu.VMEM(grid, jnp.float32),
            pltpu.SemaphoreType.DMA((2,)),
            pltpu.SemaphoreType.DMA((2,)),
        ],
        compiler_params=pltpu.CompilerParams(collective_id=0, has_side_effects=True),
    )(flags, offsets, places, speeds, pixels)
    return got.reshape(2, devices, lane_count)


def pick(data, hits):
    chosen = jnp.where(hits[:, :, None], data[..., None, :, :], jnp.zeros((), data.dtype))
    return jnp.sum(chosen, axis=-2)


def on_device(positions, velocities, block_order, flags, offsets, pixels):
    count_x = lax.axis_size("gx")
    count_y = lax.axis_size("gy")
    devices = count_x * count_y
    new_places, new_speeds = migrate(block_order, positions, velocities)
    half = lane_count // 2
    got = exchange(flags, offsets, new_places, new_speeds, pixels, count_x, count_y)
    got_values = jnp.stack([got[0, :, :half], got[0, :, half:], got[1, :, :half]], axis=1)
    got_values = got_values.reshape(devices, 3, half).transpose(0, 2, 1).reshape(devices * half, 3)
    got_pixel = got[1, :, half:].reshape(devices * half).astype(jnp.int32)
    rows = got_pixel // lane_count
    lanes = got_pixel % lane_count
    row_hits = (rows[None, :] == jnp.arange(STRIP_ROWS, dtype=jnp.int32)[:, None]).astype(jnp.bfloat16)
    lane_hits = (lanes[:, None] == jnp.arange(lane_count, dtype=jnp.int32)[None, :]).astype(jnp.bfloat16)
    spread = (got_values.astype(jnp.bfloat16)[:, :, None] * lane_hits[:, None, :]).reshape(
        devices * half, 3 * lane_count
    )
    maps = jnp.dot(row_hits, spread, preferred_element_type=jnp.float32)
    return (new_places, new_speeds, maps)


def solution(mesh):
    in_specs = (
        P(None, ("gx", "gy")),
        P(None, ("gx", "gy")),
        P(("gx", "gy"), None),
        P(("gx", "gy"), None),
        P(),
        P(None, ("gx", "gy")),
    )
    out_specs = (P(None, ("gx", "gy")), P(None, ("gx", "gy")), P(("gx", "gy"), None))
    return jax.shard_map(
        on_device, mesh=mesh, in_specs=in_specs, out_specs=out_specs, check_vma=False
    )
```

```python
import jax
import jax.numpy as jnp
from jax import lax
from jax.experimental import pallas as pl
from jax.experimental.pallas import tpu as pltpu
from jax.sharding import PartitionSpec as P

MOVERS = 2
CROSS_MAX = 5
REPLICAS = 3
STRIP_ROWS = 64


time_step = 0.05
lane_count = 128
MESH = pl.DeviceIdType.MESH


def exchange_kernel(flags_ref, offsets_ref, places_ref, speeds_ref, pixels_ref, out_ref, pixel_ref, send_ref, middle, recv, send_sems, recv_sems):
    count_x, count_y = send_ref.shape[0], send_ref.shape[1]
    x = lax.axis_index("gx")
    y = lax.axis_index("gy")
    barrier = pltpu.get_barrier_semaphore()

    def greet_y(offset, carry):
        where = (x, lax.rem(y + offset, count_y))
        pl.semaphore_signal(barrier, 1, device_id=where, device_id_type=MESH)
        return carry

    def greet_x(offset, carry):
        where = (lax.rem(x + offset, count_x), y)
        pl.semaphore_signal(barrier, 1, device_id=where, device_id_type=MESH)
        return carry

    lax.fori_loop(1, count_y, greet_y, 0)
    lax.fori_loop(1, count_x, greet_x, 0)
    first, second = fill_send(flags_ref, offsets_ref, places_ref, speeds_ref, pixels_ref, count_x * count_y)
    for row in range(count_x):
        rows = slice(row * count_y, (row + 1) * count_y)
        send_ref[row, :, 0, :] = first[rows]
        send_ref[row, :, 1, :] = second[rows]
    pl.semaphore_wait(barrier, count_x + count_y - 2)

    pltpu.make_async_copy(send_ref.at[:, y], middle.at[y], recv_sems.at[0]).start()

    def post_y(offset, carry):
        other = lax.rem(y + offset, count_y)
        pltpu.make_async_remote_copy(
            src_ref=send_ref.at[:, other],
            dst_ref=middle.at[y],
            send_sem=send_sems.at[0],
            recv_sem=recv_sems.at[0],
            device_id=(x, other),
            device_id_type=MESH,
        ).start()
        return carry

    lax.fori_loop(1, count_y, post_y, 0)
    pltpu.make_async_copy(middle, middle, recv_sems.at[0]).wait()

    pltpu.make_async_copy(middle.at[:, x], recv.at[x], recv_sems.at[1]).start()

    def post_x(offset, carry):
        other = lax.rem(x + offset, count_x)
        pltpu.make_async_remote_copy(
            src_ref=middle.at[:, other],
            dst_ref=recv.at[x],
            send_sem=send_sems.at[1],
            recv_sem=recv_sems.at[1],
            device_id=(other, y),
            device_id_type=MESH,
        ).start()
        return carry

    lax.fori_loop(1, count_x, post_x, 0)
    pltpu.make_async_copy(recv, recv, recv_sems.at[1]).wait()
    pltpu.make_async_copy(
        middle.at[pl.ds(0, count_y - 1)], middle.at[pl.ds(0, count_y - 1)], send_sems.at[0]
    ).wait()
    pltpu.make_async_copy(
        recv.at[pl.ds(0, count_x - 1)], recv.at[pl.ds(0, count_x - 1)], send_sems.at[1]
    ).wait()
    for row in range(out_ref.shape[0]):
        out_ref[row] = recv[:, :, row, :].astype(out_ref.dtype)
    pixel_ref[...] = recv[:, :, 1, :].astype(jnp.int32)


def migrate_kernel(order_ref, positions_ref, velocities_ref, places_ref, speeds_ref, outgoing, recv, send_sem, recv_sem):
    count_x = lax.axis_size("gx")
    count_y = lax.axis_size("gy")
    x = lax.axis_index("gx")
    y = lax.axis_index("gy")
    faces = (
        (lax.rem(x + 1, count_x), y),
        (lax.rem(x + count_x - 1, count_x), y),
        (x, lax.rem(y + 1, count_y)),
        (x, lax.rem(y + count_y - 1, count_y)),
    )
    barrier = pltpu.get_barrier_semaphore()
    for where in faces:
        pl.semaphore_signal(barrier, 1, device_id=where, device_id_type=MESH)

    blocks = order_ref.shape[1]
    width = lane_count
    lanes = lambda b: slice(b * width, (b + 1) * width)
    drifted = [positions_ref[:, lanes(b)] + time_step * velocities_ref[:, lanes(b)] for b in range(blocks)]
    moving = [velocities_ref[:, lanes(b)] for b in range(blocks)]

    def ordered(source, k):
        total = None
        for b in range(blocks):
            term = jnp.where(order_ref[0, k] == b, source[b], 0.0)
            total = term if total is None else total + term
        return total

    stay = 4 * MOVERS
    for k in range(stay, blocks):
        places_ref[:, lanes(k - stay)] = ordered(drifted, k)
        speeds_ref[:, lanes(k - stay)] = ordered(moving, k)
    component_row = lax.broadcasted_iota(jnp.int32, (3, width), 0)
    steps = ((0, -1.0), (0, 1.0), (1, -1.0), (1, 1.0))
    for face, (component, sign_step) in enumerate(steps):
        for j in range(MOVERS):
            k = face * MOVERS + j
            moved = ordered(drifted, k) + jnp.where(component_row == component, sign_step, 0.0)
            outgoing[face, 0:3, lanes(j)] = moved
            outgoing[face, 3:6, lanes(j)] = ordered(moving, k)
    pl.semaphore_wait(barrier, len(faces))

    copies = []
    for face, where in enumerate(faces):
        copy = pltpu.make_async_remote_copy(
            src_ref=outgoing.at[face],
            dst_ref=recv.at[face],
            send_sem=send_sem.at[face],
            recv_sem=recv_sem.at[face],
            device_id=where,
            device_id_type=MESH,
        )
        copy.start()
        copies.append(copy)
    for copy in copies:
        copy.wait()
    for face in range(len(faces)):
        for j in range(MOVERS):
            k = blocks - stay + face * MOVERS + j
            places_ref[:, lanes(k)] = recv[face, 0:3, lanes(j)]
            speeds_ref[:, lanes(k)] = recv[face, 3:6, lanes(j)]


def migrate(block_order, positions, velocities):
    smem = pl.BlockSpec(memory_space=pltpu.SMEM)
    vmem = pl.BlockSpec(memory_space=pltpu.VMEM)
    buffer = (4, 6, MOVERS * lane_count)
    return pl.pallas_call(
        migrate_kernel,
        out_shape=(
            jax.ShapeDtypeStruct(positions.shape, jnp.float32),
            jax.ShapeDtypeStruct(velocities.shape, jnp.float32),
        ),
        in_specs=[smem, vmem, vmem],
        out_specs=(vmem, vmem),
        scratch_shapes=[
            pltpu.VMEM(buffer, jnp.float32),
            pltpu.VMEM(buffer, jnp.float32),
            pltpu.SemaphoreType.DMA((4,)),
            pltpu.SemaphoreType.DMA((4,)),
        ],
        compiler_params=pltpu.CompilerParams(collective_id=1, has_side_effects=True),
    )(block_order, positions, velocities)


def fill_send(flags_ref, offsets_ref, places_ref, speeds_ref, pixels_ref, devices):
    blocks = flags_ref.shape[1]
    count_x = lax.axis_size("gx")
    count_y = lax.axis_size("gy")
    cell_x = lax.axis_index("gx").astype(jnp.float32)
    cell_y = lax.axis_index("gy").astype(jnp.float32)
    strip_size = STRIP_ROWS * lane_count
    half = lane_count // 2

    flag = [flags_ref[0, b] for b in range(blocks)]
    flagged = sum(flag)
    place, upto = [], 0
    for b in range(blocks):
        upto = upto + flag[b]
        place.append(jnp.where(flag[b] == 1, upto - 1, flagged + b - upto))
    chosen = [sum(jnp.where(place[b] == k, b, 0) for b in range(blocks)) for k in range(CROSS_MAX)]
    live = [sum(jnp.where(place[b] == k, flag[b], 0) for b in range(blocks)) for k in range(CROSS_MAX)]

    def picked(ref, k):
        total = None
        for b in range(blocks):
            block = ref[:, b * lane_count : (b + 1) * lane_count]
            term = jnp.where(chosen[k] == b, block, jnp.zeros((), block.dtype))
            total = term if total is None else total + term
        return total

    picked_pos = [picked(places_ref, k) for k in range(CROSS_MAX)]
    picked_vel = [picked(speeds_ref, k) for k in range(CROSS_MAX)]
    picked_ids = [picked(pixels_ref, k) for k in range(CROSS_MAX)]
    dest_iota = lax.broadcasted_iota(jnp.int32, (devices, lane_count), 0)
    slot_iota = lax.broadcasted_iota(jnp.int32, (lane_count, lane_count), 0)
    before = (
        lax.broadcasted_iota(jnp.int32, (lane_count, lane_count), 0)
        < lax.broadcasted_iota(jnp.int32, (lane_count, lane_count), 1)
    ).astype(jnp.bfloat16)
    nt = (((1,), (1,)), ((), ()))
    values_part = jnp.zeros((devices, lane_count), jnp.float32)
    strip_part = jnp.zeros((devices, lane_count), jnp.float32)
    lane_part = jnp.zeros((devices, lane_count), jnp.float32)
    for replica in range(REPLICAS):
        shift = [offsets_ref[replica, c].astype(jnp.float32) for c in range(3)]
        seen = jnp.zeros((devices, 1), jnp.float32)
        for k in range(CROSS_MAX):
            pos, vel, ids = picked_pos[k], picked_vel[k], picked_ids[k][replica : replica + 1]
            mask = live[k].astype(jnp.float32)
            s0 = (cell_x + pos[0:1]) / count_x + shift[0]
            s1 = (cell_y + pos[1:2]) / count_y + shift[1]
            s2 = pos[2:3] + shift[2]
            radius = s0 * s0 + s1 * s1 + s2 * s2
            weight = 1.0 / (1.0 + radius)
            radial = (vel[0:1] * s0 + vel[1:2] * s1 + vel[2:3] * s2) / jnp.sqrt(1.0 + radius)
            energy = (vel[0:1] * vel[0:1] + vel[1:2] * vel[1:2] + vel[2:3] * vel[2:3]) / 3.0
            value = [
                (weight * mask).astype(jnp.bfloat16).astype(jnp.float32),
                (weight * radial * mask).astype(jnp.bfloat16).astype(jnp.float32),
                (weight * energy * mask).astype(jnp.bfloat16).astype(jnp.float32),
            ]
            dest = ids // strip_size
            inside = ids % strip_size
            dest_hits = (dest == dest_iota).astype(jnp.bfloat16)
            counted = seen + jnp.dot(dest_hits, before, preferred_element_type=jnp.float32)
            rank = jnp.sum(dest_hits.astype(jnp.float32) * counted, axis=0, keepdims=True)
            seen = seen + jnp.sum(dest_hits.astype(jnp.float32), axis=1, keepdims=True)
            slot = rank.astype(jnp.int32) + replica * blocks
            low = slot_iota == slot
            high = slot_iota == slot + half
            first = (jnp.where(low, value[0], 0.0) + jnp.where(high, value[1], 0.0)).astype(jnp.bfloat16)
            second = jnp.where(low, value[2], 0.0) + jnp.where(high, (inside // lane_count).astype(jnp.float32), 0.0)
            third = jnp.where(high, (inside % lane_count).astype(jnp.float32), 0.0)
            values_part += lax.dot_general(dest_hits, first, nt, preferred_element_type=jnp.float32)
            strip_part += lax.dot_general(
                dest_hits, second.astype(jnp.bfloat16), nt, preferred_element_type=jnp.float32
            )
            lane_part += lax.dot_general(
                dest_hits, third.astype(jnp.bfloat16), nt, preferred_element_type=jnp.float32
            )
    scale = jnp.where(lax.broadcasted_iota(jnp.int32, (1, lane_count), 1) < half, 1.0, float(lane_count))
    return values_part, strip_part * scale + lane_part


def exchange(flags, offsets, places, speeds, pixels, count_x, count_y):
    devices = count_x * count_y
    grid = (count_x, count_y, 2, lane_count)
    middle = (count_y, count_x, 2, lane_count)
    smem = pl.BlockSpec(memory_space=pltpu.SMEM)
    vmem = pl.BlockSpec(memory_space=pltpu.VMEM)
    got = pl.pallas_call(
        exchange_kernel,
        out_shape=(
            jax.ShapeDtypeStruct((2, count_x, count_y, lane_count), jnp.bfloat16),
            jax.ShapeDtypeStruct((count_x, count_y, lane_count), jnp.int32),
        ),
        in_specs=[smem, smem, vmem, vmem, vmem],
        out_specs=(vmem, vmem),
        scratch_shapes=[
            pltpu.VMEM(grid, jnp.float32),
            pltpu.VMEM(middle, jnp.float32),
            pltpu.VMEM(grid, jnp.float32),
            pltpu.SemaphoreType.DMA((2,)),
            pltpu.SemaphoreType.DMA((2,)),
        ],
        compiler_params=pltpu.CompilerParams(collective_id=0, has_side_effects=True),
    )(flags, offsets, places, speeds, pixels)
    return got[0].reshape(2, devices, lane_count), got[1].reshape(devices, lane_count)


def pick(data, hits):
    chosen = jnp.where(hits[:, :, None], data[..., None, :, :], jnp.zeros((), data.dtype))
    return jnp.sum(chosen, axis=-2)


def on_device(positions, velocities, block_order, flags, offsets, pixels):
    count_x = lax.axis_size("gx")
    count_y = lax.axis_size("gy")
    devices = count_x * count_y
    new_places, new_speeds = migrate(block_order, positions, velocities)
    half = lane_count // 2
    got, got_pixel = exchange(flags, offsets, new_places, new_speeds, pixels, count_x, count_y)
    got_values = jnp.stack([got[0, :, :half], got[0, :, half:], got[1, :, :half]], axis=1)
    got_values = got_values.reshape(devices, 3, half).transpose(0, 2, 1).reshape(devices * half, 3)
    got_pixel = got_pixel[:, half:].reshape(devices * half)
    rows = got_pixel // lane_count
    lanes = got_pixel % lane_count
    row_hits = (rows[None, :] == jnp.arange(STRIP_ROWS, dtype=jnp.int32)[:, None]).astype(jnp.bfloat16)
    lane_hits = (lanes[:, None] == jnp.arange(lane_count, dtype=jnp.int32)[None, :]).astype(jnp.bfloat16)
    spread = (got_values.astype(jnp.bfloat16)[:, :, None] * lane_hits[:, None, :]).reshape(
        devices * half, 3 * lane_count
    )
    maps = jnp.dot(row_hits, spread, preferred_element_type=jnp.float32)
    return (new_places, new_speeds, maps)


def solution(mesh):
    in_specs = (
        P(None, ("gx", "gy")),
        P(None, ("gx", "gy")),
        P(("gx", "gy"), None),
        P(("gx", "gy"), None),
        P(),
        P(None, ("gx", "gy")),
    )
    out_specs = (P(None, ("gx", "gy")), P(None, ("gx", "gy")), P(("gx", "gy"), None))
    return jax.shard_map(
        on_device, mesh=mesh, in_specs=in_specs, out_specs=out_specs, check_vma=False
    )
```

```python
import jax
import jax.numpy as jnp
from jax import lax
from jax.experimental import pallas as pl
from jax.experimental.pallas import tpu as pltpu
from jax.sharding import PartitionSpec as P

MOVERS = 2
CROSS_MAX = 5
REPLICAS = 3
STRIP_ROWS = 64


time_step = 0.05
lane_count = 128
MESH = pl.DeviceIdType.MESH


def exchange_kernel(flags_ref, offsets_ref, places_ref, speeds_ref, pixels_ref, out_ref, send_ref, middle, recv, send_sems, recv_sems):
    count_x, count_y = send_ref.shape[0], send_ref.shape[1]
    x = lax.axis_index("gx")
    y = lax.axis_index("gy")
    barrier = pltpu.get_barrier_semaphore()

    def greet_y(offset, carry):
        where = (x, lax.rem(y + offset, count_y))
        pl.semaphore_signal(barrier, 1, device_id=where, device_id_type=MESH)
        return carry

    def greet_x(offset, carry):
        where = (lax.rem(x + offset, count_x), y)
        pl.semaphore_signal(barrier, 1, device_id=where, device_id_type=MESH)
        return carry

    for offset in range(1, count_y):
        greet_y(offset, None)
    for offset in range(1, count_x):
        greet_x(offset, None)
    first, second = fill_send(flags_ref, offsets_ref, places_ref, speeds_ref, pixels_ref, count_x * count_y)
    for row in range(count_x):
        rows = slice(row * count_y, (row + 1) * count_y)
        send_ref[row, :, 0, :] = first[rows]
        send_ref[row, :, 1, :] = second[rows]
    pl.semaphore_wait(barrier, count_x + count_y - 2)

    pltpu.make_async_copy(send_ref.at[:, y], middle.at[y], recv_sems.at[0]).start()

    def post_y(offset, carry):
        other = lax.rem(y + offset, count_y)
        pltpu.make_async_remote_copy(
            src_ref=send_ref.at[:, other],
            dst_ref=middle.at[y],
            send_sem=send_sems.at[0],
            recv_sem=recv_sems.at[0],
            device_id=(x, other),
            device_id_type=MESH,
        ).start()
        return carry

    for offset in range(1, count_y):
        post_y(offset, None)
    pltpu.make_async_copy(middle, middle, recv_sems.at[0]).wait()

    pltpu.make_async_copy(middle.at[:, x], recv.at[x], recv_sems.at[1]).start()

    def post_x(offset, carry):
        other = lax.rem(x + offset, count_x)
        pltpu.make_async_remote_copy(
            src_ref=middle.at[:, other],
            dst_ref=recv.at[x],
            send_sem=send_sems.at[1],
            recv_sem=recv_sems.at[1],
            device_id=(other, y),
            device_id_type=MESH,
        ).start()
        return carry

    for offset in range(1, count_x):
        post_x(offset, None)
    pltpu.make_async_copy(recv, recv, recv_sems.at[1]).wait()
    pltpu.make_async_copy(
        middle.at[pl.ds(0, count_y - 1)], middle.at[pl.ds(0, count_y - 1)], send_sems.at[0]
    ).wait()
    pltpu.make_async_copy(
        recv.at[pl.ds(0, count_x - 1)], recv.at[pl.ds(0, count_x - 1)], send_sems.at[1]
    ).wait()
    for row in range(out_ref.shape[0]):
        out_ref[row] = recv[:, :, row, :]


def migrate_kernel(order_ref, positions_ref, velocities_ref, places_ref, speeds_ref, outgoing, recv, send_sem, recv_sem):
    count_x = lax.axis_size("gx")
    count_y = lax.axis_size("gy")
    x = lax.axis_index("gx")
    y = lax.axis_index("gy")
    faces = (
        (lax.rem(x + 1, count_x), y),
        (lax.rem(x + count_x - 1, count_x), y),
        (x, lax.rem(y + 1, count_y)),
        (x, lax.rem(y + count_y - 1, count_y)),
    )
    barrier = pltpu.get_barrier_semaphore()
    for where in faces:
        pl.semaphore_signal(barrier, 1, device_id=where, device_id_type=MESH)

    blocks = order_ref.shape[1]
    width = lane_count
    lanes = lambda b: slice(b * width, (b + 1) * width)
    drifted = [positions_ref[:, lanes(b)] + time_step * velocities_ref[:, lanes(b)] for b in range(blocks)]
    moving = [velocities_ref[:, lanes(b)] for b in range(blocks)]

    def ordered(source, k):
        total = None
        for b in range(blocks):
            term = jnp.where(order_ref[0, k] == b, source[b], 0.0)
            total = term if total is None else total + term
        return total

    stay = 4 * MOVERS
    for k in range(stay, blocks):
        places_ref[:, lanes(k - stay)] = ordered(drifted, k)
        speeds_ref[:, lanes(k - stay)] = ordered(moving, k)
    component_row = lax.broadcasted_iota(jnp.int32, (3, width), 0)
    steps = ((0, -1.0), (0, 1.0), (1, -1.0), (1, 1.0))
    for face, (component, sign_step) in enumerate(steps):
        for j in range(MOVERS):
            k = face * MOVERS + j
            moved = ordered(drifted, k) + jnp.where(component_row == component, sign_step, 0.0)
            outgoing[face, 0:3, lanes(j)] = moved
            outgoing[face, 3:6, lanes(j)] = ordered(moving, k)
    pl.semaphore_wait(barrier, len(faces))

    copies = []
    for face, where in enumerate(faces):
        copy = pltpu.make_async_remote_copy(
            src_ref=outgoing.at[face],
            dst_ref=recv.at[face],
            send_sem=send_sem.at[face],
            recv_sem=recv_sem.at[face],
            device_id=where,
            device_id_type=MESH,
        )
        copy.start()
        copies.append(copy)
    for copy in copies:
        copy.wait()
    for face in range(len(faces)):
        for j in range(MOVERS):
            k = blocks - stay + face * MOVERS + j
            places_ref[:, lanes(k)] = recv[face, 0:3, lanes(j)]
            speeds_ref[:, lanes(k)] = recv[face, 3:6, lanes(j)]


def migrate(block_order, positions, velocities):
    smem = pl.BlockSpec(memory_space=pltpu.SMEM)
    vmem = pl.BlockSpec(memory_space=pltpu.VMEM)
    buffer = (4, 6, MOVERS * lane_count)
    return pl.pallas_call(
        migrate_kernel,
        out_shape=(
            jax.ShapeDtypeStruct(positions.shape, jnp.float32),
            jax.ShapeDtypeStruct(velocities.shape, jnp.float32),
        ),
        in_specs=[smem, vmem, vmem],
        out_specs=(vmem, vmem),
        scratch_shapes=[
            pltpu.VMEM(buffer, jnp.float32),
            pltpu.VMEM(buffer, jnp.float32),
            pltpu.SemaphoreType.DMA((4,)),
            pltpu.SemaphoreType.DMA((4,)),
        ],
        compiler_params=pltpu.CompilerParams(collective_id=1, has_side_effects=True),
    )(block_order, positions, velocities)


def fill_send(flags_ref, offsets_ref, places_ref, speeds_ref, pixels_ref, devices):
    blocks = flags_ref.shape[1]
    count_x = lax.axis_size("gx")
    count_y = lax.axis_size("gy")
    cell_x = lax.axis_index("gx").astype(jnp.float32)
    cell_y = lax.axis_index("gy").astype(jnp.float32)
    strip_size = STRIP_ROWS * lane_count
    half = lane_count // 2

    flag = [flags_ref[0, b] for b in range(blocks)]
    flagged = sum(flag)
    place, upto = [], 0
    for b in range(blocks):
        upto = upto + flag[b]
        place.append(jnp.where(flag[b] == 1, upto - 1, flagged + b - upto))
    chosen = [sum(jnp.where(place[b] == k, b, 0) for b in range(blocks)) for k in range(CROSS_MAX)]
    live = [sum(jnp.where(place[b] == k, flag[b], 0) for b in range(blocks)) for k in range(CROSS_MAX)]

    def picked(ref, k):
        total = None
        for b in range(blocks):
            block = ref[:, b * lane_count : (b + 1) * lane_count]
            term = jnp.where(chosen[k] == b, block, jnp.zeros((), block.dtype))
            total = term if total is None else total + term
        return total

    picked_pos = [picked(places_ref, k) for k in range(CROSS_MAX)]
    picked_vel = [picked(speeds_ref, k) for k in range(CROSS_MAX)]
    picked_ids = [picked(pixels_ref, k) for k in range(CROSS_MAX)]
    dest_iota = lax.broadcasted_iota(jnp.int32, (devices, lane_count), 0)
    slot_iota = lax.broadcasted_iota(jnp.int32, (lane_count, lane_count), 0)
    before = (
        lax.broadcasted_iota(jnp.int32, (lane_count, lane_count), 0)
        < lax.broadcasted_iota(jnp.int32, (lane_count, lane_count), 1)
    ).astype(jnp.bfloat16)
    nt = (((1,), (1,)), ((), ()))
    values_part = jnp.zeros((devices, lane_count), jnp.float32)
    strip_part = jnp.zeros((devices, lane_count), jnp.float32)
    lane_part = jnp.zeros((devices, lane_count), jnp.float32)
    for replica in range(REPLICAS):
        shift = [offsets_ref[replica, c].astype(jnp.float32) for c in range(3)]
        seen = jnp.zeros((devices, 1), jnp.float32)
        for k in range(CROSS_MAX):
            pos, vel, ids = picked_pos[k], picked_vel[k], picked_ids[k][replica : replica + 1]
            mask = live[k].astype(jnp.float32)
            s0 = (cell_x + pos[0:1]) / count_x + shift[0]
            s1 = (cell_y + pos[1:2]) / count_y + shift[1]
            s2 = pos[2:3] + shift[2]
            radius = s0 * s0 + s1 * s1 + s2 * s2
            weight = 1.0 / (1.0 + radius)
            radial = (vel[0:1] * s0 + vel[1:2] * s1 + vel[2:3] * s2) / jnp.sqrt(1.0 + radius)
            energy = (vel[0:1] * vel[0:1] + vel[1:2] * vel[1:2] + vel[2:3] * vel[2:3]) / 3.0
            value = [
                (weight * mask).astype(jnp.bfloat16).astype(jnp.float32),
                (weight * radial * mask).astype(jnp.bfloat16).astype(jnp.float32),
                (weight * energy * mask).astype(jnp.bfloat16).astype(jnp.float32),
            ]
            dest = ids // strip_size
            inside = ids % strip_size
            dest_hits = (dest == dest_iota).astype(jnp.bfloat16)
            counted = seen + jnp.dot(dest_hits, before, preferred_element_type=jnp.float32)
            rank = jnp.sum(dest_hits.astype(jnp.float32) * counted, axis=0, keepdims=True)
            seen = seen + jnp.sum(dest_hits.astype(jnp.float32), axis=1, keepdims=True)
            slot = rank.astype(jnp.int32) + replica * blocks
            low = slot_iota == slot
            high = slot_iota == slot + half
            first = (jnp.where(low, value[0], 0.0) + jnp.where(high, value[1], 0.0)).astype(jnp.bfloat16)
            second = jnp.where(low, value[2], 0.0) + jnp.where(high, (inside // lane_count).astype(jnp.float32), 0.0)
            third = jnp.where(high, (inside % lane_count).astype(jnp.float32), 0.0)
            values_part += lax.dot_general(dest_hits, first, nt, preferred_element_type=jnp.float32)
            strip_part += lax.dot_general(
                dest_hits, second.astype(jnp.bfloat16), nt, preferred_element_type=jnp.float32
            )
            lane_part += lax.dot_general(
                dest_hits, third.astype(jnp.bfloat16), nt, preferred_element_type=jnp.float32
            )
    scale = jnp.where(lax.broadcasted_iota(jnp.int32, (1, lane_count), 1) < half, 1.0, float(lane_count))
    return values_part, strip_part * scale + lane_part


def exchange(flags, offsets, places, speeds, pixels, count_x, count_y):
    devices = count_x * count_y
    grid = (count_x, count_y, 2, lane_count)
    middle = (count_y, count_x, 2, lane_count)
    smem = pl.BlockSpec(memory_space=pltpu.SMEM)
    vmem = pl.BlockSpec(memory_space=pltpu.VMEM)
    got = pl.pallas_call(
        exchange_kernel,
        out_shape=jax.ShapeDtypeStruct((2, count_x, count_y, lane_count), jnp.float32),
        in_specs=[smem, smem, vmem, vmem, vmem],
        out_specs=vmem,
        scratch_shapes=[
            pltpu.VMEM(grid, jnp.float32),
            pltpu.VMEM(middle, jnp.float32),
            pltpu.VMEM(grid, jnp.float32),
            pltpu.SemaphoreType.DMA((2,)),
            pltpu.SemaphoreType.DMA((2,)),
        ],
        compiler_params=pltpu.CompilerParams(collective_id=0, has_side_effects=True),
    )(flags, offsets, places, speeds, pixels)
    return got.reshape(2, devices, lane_count)


def pick(data, hits):
    chosen = jnp.where(hits[:, :, None], data[..., None, :, :], jnp.zeros((), data.dtype))
    return jnp.sum(chosen, axis=-2)


def on_device(positions, velocities, block_order, flags, offsets, pixels):
    count_x = lax.axis_size("gx")
    count_y = lax.axis_size("gy")
    devices = count_x * count_y
    new_places, new_speeds = migrate(block_order, positions, velocities)
    half = lane_count // 2
    got = exchange(flags, offsets, new_places, new_speeds, pixels, count_x, count_y)
    got_values = jnp.stack([got[0, :, :half], got[0, :, half:], got[1, :, :half]], axis=1)
    got_values = got_values.reshape(devices, 3, half).transpose(0, 2, 1).reshape(devices * half, 3)
    got_pixel = got[1, :, half:].reshape(devices * half).astype(jnp.int32)
    rows = got_pixel // lane_count
    lanes = got_pixel % lane_count
    row_hits = (rows[None, :] == jnp.arange(STRIP_ROWS, dtype=jnp.int32)[:, None]).astype(jnp.bfloat16)
    lane_hits = (lanes[:, None] == jnp.arange(lane_count, dtype=jnp.int32)[None, :]).astype(jnp.bfloat16)
    spread = (got_values.astype(jnp.bfloat16)[:, :, None] * lane_hits[:, None, :]).reshape(
        devices * half, 3 * lane_count
    )
    maps = jnp.dot(row_hits, spread, preferred_element_type=jnp.float32)
    return (new_places, new_speeds, maps)


def solution(mesh):
    in_specs = (
        P(None, ("gx", "gy")),
        P(None, ("gx", "gy")),
        P(("gx", "gy"), None),
        P(("gx", "gy"), None),
        P(),
        P(None, ("gx", "gy")),
    )
    out_specs = (P(None, ("gx", "gy")), P(None, ("gx", "gy")), P(("gx", "gy"), None))
    return jax.shard_map(
        on_device, mesh=mesh, in_specs=in_specs, out_specs=out_specs, check_vma=False
    )
```
